32 devices in a mesh: groups: 2 (over y), seq: 16 (over z, x, core).
Axes of the slice: x: 2, y: 2, z: 4, core: 2. Of those that a mesh axis runs over, the one named last changes fastest.
Arguments:
- query_src: bfloat16 [4096, 2048], P(('groups', 'seq')), parts along dimension 0, may hold values from -6 to 6
- key_src: bfloat16 [4096, 2048], P(('groups', 'seq')), parts along dimension 0, may hold values from -6 to 6
- value_src: bfloat16 [4096, 2048], P(('groups', 'seq')), parts along dimension 0, may hold values from -6 to 6
- up_query: bfloat16 [4096, 2048], P(('groups', 'seq')), parts along dimension 0, may hold values from -6 to 6
- query_gain: float32 [2048], replicated, may hold values from 1.2 to 2.4
- key_gain: float32 [2048], replicated, may hold values from 1.2 to 2.4
- up_gain: float32 [2048], replicated, may hold values from 1.5 to 5
Outputs:
- upsampled: bfloat16 [4096, 2048], P(('groups', 'seq')), parts along dimension 0
The draws below stay inside these ranges and needn't reach their ends.
There are 2 independent parts, one for each index of `groups`. The reference program is written for one: setup_inputs(seed, part) draws one part's arguments, and reference() takes and returns one part's arrays. A program takes and returns all parts, laid end to end along the dimension named above; an argument that names none is the same for every part. Nothing has to cross between parts.
All inputs are finite; a program needn't handle non-finite values.
Results may differ from the reference program's by a relative error of at most 0.002.
The reference program's roundings to bfloat16 on the way count: a program that leaves them out, or rounds other values in their place, can miss the bound.
Values may be sent and summed in bfloat16 or wider, within the bound.
No kernel may reach another device: no remote copies, remote signals or barrier semaphores. Data moves between devices by JAX's collectives and lax.ppermute only.
A program may use at most 128 MiB of HBM per device.

```python
import math
import jax
import jax.numpy as jnp
from jax import lax

HEADS = 16
HDIM = 128
SHORT = 4
SHIFT = 3
HD = 2048
TOKENS = 2048


def block_scale(key, extent, cuts, low, largest):
    def one(axis_at, parts):
        draws = jax.random.uniform(jax.random.fold_in(jax.random.fold_in(key, 6), axis_at), (parts,), jnp.float32, low / len(cuts), largest / len(cuts))
        return jnp.repeat(jnp.exp(draws), extent[axis_at] // parts).reshape((-1,) + (1,) * (len(extent) - axis_at - 1))

    level = one(*cuts[0])
    for cut in cuts[1:]:
        level = level * one(*cut)
    return level


def normal_values(key, extent, deviation, limit, cuts=(), dtype=jnp.bfloat16):
    entries = deviation * jax.random.normal(key, extent, jnp.float32)
    if cuts:
        entries = entries * block_scale(key, extent, cuts, -0.22, 0.18)
    return jnp.clip(entries, -limit, limit).astype(dtype)


def setup_inputs(seed: int = 0, part: int = 0) -> dict:
    arg_keys = jax.random.split(jax.random.key(seed), 8)
    part_keys = jax.random.split(jax.random.fold_in(arg_keys[7], part), 8)
    return {
        "query_src": normal_values(part_keys[0], (TOKENS, HD), 1.0, 6.0, ((0, 16),)),
        "key_src": normal_values(part_keys[1], (TOKENS, HD), 1.0, 6.0, ((0, 16),)),
        "value_src": normal_values(part_keys[2], (TOKENS, HD), 1.0, 6.0, ((0, 16),)),
        "up_query": normal_values(part_keys[3], (TOKENS, HD), 1.0, 6.0, ((0, 16),)),
        "query_gain": jnp.clip(jnp.exp(jax.random.uniform(arg_keys[4], (HD,), jnp.float32, math.log(1.2), math.log(2.4))), 1.2, 2.4),
        "key_gain": jnp.clip(jnp.exp(jax.random.uniform(arg_keys[5], (HD,), jnp.float32, math.log(1.2), math.log(2.4))), 1.2, 2.4),
        "up_gain": jnp.clip(jnp.exp(jax.random.uniform(arg_keys[6], (HD,), jnp.float32, math.log(1.5), math.log(5.0))), 1.5, 5.0),
    }


epsilon = 1e-06

def head_norm(values, gain_vector):
    row_count = values.shape[0]
    by_head = values.reshape(row_count, HEADS, HDIM)
    inverse_rms = lax.rsqrt(lax.optimization_barrier(jnp.mean(by_head * by_head, axis=2, keepdims=True)) + epsilon)
    return (by_head * inverse_rms * gain_vector.reshape(1, HEADS, HDIM)).reshape(row_count, HEADS * HDIM)

def pool_rows(source):
    widened = source.astype(jnp.float32)
    width = widened.shape[1]
    shifted = jnp.concatenate([jnp.zeros((SHIFT, width), jnp.float32), widened[:widened.shape[0] - SHIFT]], axis=0)
    return lax.optimization_barrier(jnp.mean(shifted.reshape(-1, SHORT, width), axis=1))

def attend_rows(queries, key_rows, value_rows, visible):
    scores = jnp.dot(queries, key_rows.T, preferred_element_type=jnp.float32) / math.sqrt(HDIM)
    exponent = jnp.where(visible, jnp.exp(scores), 0.0)
    denominator = lax.optimization_barrier(jnp.sum(exponent, axis=1, keepdims=True))
    numerator = jnp.dot(exponent.astype(jnp.bfloat16), value_rows, preferred_element_type=jnp.float32)
    return numerator / denominator

def split_heads(matrix, length):
    return jnp.transpose(matrix.reshape(length, HEADS, HDIM), (1, 0, 2))

def reference(query_src, key_src, value_src, up_query, query_gain, key_gain, up_gain):
    short_query = head_norm(pool_rows(query_src), query_gain).astype(jnp.bfloat16)
    short_key = head_norm(pool_rows(key_src), key_gain).astype(jnp.bfloat16)
    short_value = pool_rows(value_src).astype(jnp.bfloat16)
    row_count = short_query.shape[0]
    token_count = up_query.shape[0]
    row_pos = jnp.arange(row_count)
    short_visible = row_pos[None, :] <= row_pos[:, None]

    def short_head(operands):
        head_query, head_key, head_value = operands
        attended = attend_rows(head_query, head_key, head_value, short_visible)
        inverse_rms = lax.rsqrt(lax.optimization_barrier(jnp.mean(attended * attended, axis=1, keepdims=True)) + epsilon)
        return (attended * inverse_rms).astype(jnp.bfloat16)
    memory = lax.map(short_head, (split_heads(short_query, row_count), split_heads(short_key, row_count), split_heads(short_value, row_count)))
    up_heads = split_heads(head_norm(up_query.astype(jnp.float32), up_gain).astype(jnp.bfloat16), token_count)
    token_block = token_count // 8
    row_block = row_count // 8
    pieces = []
    for block_index in range(8):
        key_count = (block_index + 1) * row_block
        tok_pos = jnp.arange(block_index * token_block, (block_index + 1) * token_block)
        visible = jnp.arange(key_count)[None, :] * SHORT <= tok_pos[:, None]
        query_part = up_heads[:, block_index * token_block:(block_index + 1) * token_block]

        def up_head(operands, visible=visible, key_count=key_count):
            head_query, head_memory = operands
            return attend_rows(head_query, head_memory[:key_count], head_memory[:key_count], visible)
        pieces.append(lax.map(up_head, (query_part, memory)))
    combined = jnp.concatenate(pieces, axis=1)
    return jnp.transpose(combined, (1, 0, 2)).reshape(token_count, HEADS * HDIM).astype(jnp.bfloat16)
```

```python
import functools
import math

import jax
import jax.numpy as jnp
from jax import lax
from jax.experimental import pallas as pl
from jax.experimental.pallas import tpu as pltpu
from jax.sharding import PartitionSpec as P

HEADS = 16
HDIM = 128
SHORT = 4
SHIFT = 3


epsilon = 1e-06


def shifted(value, axis, steps):
    count = lax.axis_size(axis)
    leading, last = (max(0, -steps), min(count, count - steps))
    return lax.ppermute(value, axis, [(source, source + steps) for source in range(leading, last)])


def head_norm(values, gain_vector):
    row_count = values.shape[0]
    by_head = values.reshape(row_count, HEADS, HDIM)
    inverse_rms = lax.rsqrt(jnp.mean(by_head * by_head, axis=2, keepdims=True) + epsilon)
    return (by_head * inverse_rms * gain_vector.reshape(1, HEADS, HDIM)).reshape(
        row_count, HEADS * HDIM
    )


def row_norm(values):
    return values * lax.rsqrt(jnp.mean(values * values, axis=-1, keepdims=True) + epsilon)


def pooled_rows(source, edge_rows):
    widened = jnp.concatenate([edge_rows, source[: source.shape[0] - SHIFT]], axis=0).astype(
        jnp.float32
    )
    return jnp.mean(widened.reshape(-1, SHORT, widened.shape[1]), axis=1)


def blocked_attention(queries, query_limit, key_rows, value_rows, key_positions, block_size):
    head_count, query_count, head_size = queries.shape
    block_total = key_rows.shape[1] // block_size
    ceiling = jnp.max(query_limit)

    def visit_block(block_index, totals):
        offset = block_index * block_size
        block_pos = lax.dynamic_slice_in_dim(key_positions, offset, block_size, 0)

        def compute(state):
            numer_in, denom_in = state
            key_block = lax.dynamic_slice_in_dim(key_rows, offset, block_size, 1)
            value_block = lax.dynamic_slice_in_dim(value_rows, offset, block_size, 1)
            scores = jnp.einsum(
                "hqd,hkd->hqk", queries, key_block, preferred_element_type=jnp.float32
            ) / math.sqrt(HDIM)
            visible = block_pos[None, :] <= query_limit[:, None]
            exponent = jnp.where(visible[None], jnp.exp(scores), 0.0)
            denom_out = denom_in + jnp.sum(exponent, axis=2)
            numer_out = numer_in + jnp.einsum(
                "hqk,hkd->hqd",
                exponent.astype(jnp.bfloat16),
                value_block,
                preferred_element_type=jnp.float32,
            )
            return (numer_out, denom_out)

        return lax.cond(jnp.min(block_pos) <= ceiling, compute, lambda state: state, totals)

    initial = (
        jnp.zeros((head_count, query_count, head_size), jnp.float32),
        jnp.zeros((head_count, query_count), jnp.float32),
    )
    numerator, denominator = lax.fori_loop(0, block_total, visit_block, initial)
    return numerator / denominator[:, :, None]


def spread_heads(matrices, row_count, block_count, device_count):
    count = len(matrices)
    joined = jnp.stack(matrices).reshape(count, row_count, HEADS, HDIM)
    joined = jnp.transpose(joined, (2, 0, 1, 3)).reshape(HEADS, 1, count * row_count, HDIM)
    return jnp.broadcast_to(joined, (HEADS, block_count, count * row_count, HDIM)).reshape(
        device_count, count * row_count, HDIM
    )


def split_pieces(matrix, row_count, block_count, device_count):
    piece = row_count // block_count
    parted = matrix.reshape(block_count, piece, HEADS, HDIM)
    return jnp.transpose(parted, (2, 0, 1, 3)).reshape(device_count, piece, HDIM)


def head_exchange(query_src, key_src, value_src, up_query, query_gain, key_gain, up_gain):
    device_count = lax.axis_size("seq")
    device_index = lax.axis_index("seq")
    block_count = device_count // HEADS
    block_index = device_index % block_count
    token_count = query_src.shape[0]
    edges = jnp.stack(
        [
            query_src[token_count - SHIFT :],
            key_src[token_count - SHIFT :],
            value_src[token_count - SHIFT :],
        ]
    )
    edges = shifted(edges, "seq", 1)
    short_query = head_norm(pooled_rows(query_src, edges[0]), query_gain).astype(jnp.bfloat16)
    short_key = head_norm(pooled_rows(key_src, edges[1]), key_gain).astype(jnp.bfloat16)
    short_value = pooled_rows(value_src, edges[2]).astype(jnp.bfloat16)
    row_count = short_query.shape[0]
    up_heads = head_norm(up_query.astype(jnp.float32), up_gain).astype(jnp.bfloat16)
    row_total = row_count * device_count
    key_block = math.gcd(512, row_total)
    row_positions = jnp.arange(row_total, dtype=jnp.int32)
    device_rows = jnp.arange(device_count, dtype=jnp.int32)[:, None]
    qkv_out = spread_heads(
        [short_query, short_key, short_value], row_count, block_count, device_count
    )
    up_out = split_pieces(up_heads, token_count, block_count, device_count)
    arrived, own_up = (
        lax.all_to_all(qkv_out, "seq", split_axis=0, concat_axis=0, tiled=True),
        lax.all_to_all(up_out, "seq", split_axis=0, concat_axis=0, tiled=True),
    )
    all_query = arrived[:, :row_count].reshape(row_total, HDIM)
    all_key = arrived[:, row_count : 2 * row_count].reshape(row_total, HDIM)
    all_value = arrived[:, 2 * row_count :].reshape(row_total, HDIM)

    def fill_block(index_now, memory_now):
        offset = index_now * key_block
        block_query = lax.dynamic_slice_in_dim(all_query, offset, key_block, 0)[None]
        limits = offset + jnp.arange(key_block, dtype=jnp.int32)
        attended = blocked_attention(
            block_query, limits, all_key[None], all_value[None], row_positions, key_block
        )[0]
        return lax.dynamic_update_slice_in_dim(
            memory_now, row_norm(attended).astype(jnp.bfloat16), offset, 0
        )

    memory = lax.fori_loop(
        0, row_total // key_block, fill_block, jnp.zeros((row_total, HDIM), jnp.bfloat16)
    )
    token_piece = token_count // block_count
    own_tokens = (
        device_rows * token_count
        + block_index * token_piece
        + jnp.arange(token_piece, dtype=jnp.int32)[None, :]
    ).reshape(-1)
    own_up = own_up.reshape(1, device_count * token_piece, HDIM)
    result = blocked_attention(
        own_up, own_tokens // SHORT, memory[None], memory[None], row_positions, key_block
    )[0]
    result = result.astype(jnp.bfloat16).reshape(device_count, token_piece, HDIM)
    returned = lax.all_to_all(result, "seq", split_axis=0, concat_axis=0, tiled=True)
    output_heads = returned.reshape(HEADS, token_count, HDIM)
    return jnp.transpose(output_heads, (1, 0, 2)).reshape(token_count, HEADS * HDIM)


EDGE_ROWS = 16


def rms_rows(values):
    return values * lax.rsqrt(jnp.mean(values * values, axis=-1, keepdims=True) + epsilon)


def select_matrix(tokens, rows, slot):
    row = lax.broadcasted_iota(jnp.int32, (rows + EDGE_ROWS, tokens), 0)
    col = lax.broadcasted_iota(jnp.int32, (rows + EDGE_ROWS, tokens), 1)
    pooled = (row < rows) & (col <= SHORT * row) & (col >= SHORT * row - SHIFT)
    weight = jnp.where(row == 0, 1.0, 1.0 / SHORT)
    edge = (row >= rows + slot * SHIFT) & (row < rows + (slot + 1) * SHIFT)
    edge = edge & (col == tokens - SHIFT + row - rows - slot * SHIFT)
    return jnp.where(pooled, weight, jnp.where(edge, 1.0, 0.0)).astype(jnp.bfloat16)


def pool_kernel(query_ref, key_ref, value_ref, query_gain_ref, key_gain_ref, out_ref):
    tokens, width = query_ref.shape
    rows = tokens // SHORT
    picked = [
        jnp.dot(select_matrix(tokens, rows, slot), ref[...], preferred_element_type=jnp.float32)
        for slot, ref in enumerate((query_ref, key_ref, value_ref))
    ]
    first = lax.broadcasted_iota(jnp.int32, (rows, HDIM), 0) == 0
    gains = (query_gain_ref, key_gain_ref)
    for head in range(width // HDIM):
        columns = slice(head * HDIM, (head + 1) * HDIM)
        for slot in range(3):
            part = picked[slot][:rows, columns]
            if slot < 2:
                part = jnp.where(first, part, rms_rows(part) * gains[slot][:, columns])
            out_ref[head, slot * rows : (slot + 1) * rows, :] = part.astype(jnp.bfloat16)
        edge = sum(values[rows:, columns] for values in picked)
        out_ref[head, 3 * rows :, :] = edge.astype(jnp.bfloat16)


def pool_inputs(query_src, key_src, value_src, query_gain, key_gain, heads_at_once):
    tokens, columns = query_src.shape
    width = heads_at_once * HDIM
    depth = 3 * (tokens // SHORT) + EDGE_ROWS
    source = pl.BlockSpec((tokens, width), lambda step: (0, step))
    gain = pl.BlockSpec((1, width), lambda step: (0, step))
    return pl.pallas_call(
        pool_kernel,
        grid=(columns // width,),
        in_specs=[source, source, source, gain, gain],
        out_specs=pl.BlockSpec((heads_at_once, depth, HDIM), lambda step: (step, 0, 0)),
        out_shape=jax.ShapeDtypeStruct((columns // HDIM, depth, HDIM), jnp.bfloat16),
    )(query_src, key_src, value_src, query_gain.reshape(1, -1), key_gain.reshape(1, -1))


def masked_exp(scores, visible):
    exponent = jnp.exp(scores * (1.0 / math.sqrt(HDIM)))
    return exponent if visible is None else jnp.where(visible, exponent, 0.0)


def across(left, right):
    return lax.dot_general(
        left, right, (((1,), (1,)), ((), ())), preferred_element_type=jnp.float32
    )


def short_kernel(block, arrived_ref, query_gain_ref, key_gain_ref, memory_ref):
    count, depth, _ = arrived_ref.shape
    rows = (depth - EDGE_ROWS) // 3
    head = lax.axis_index("seq")
    edges = arrived_ref[:, 3 * rows :, :].astype(jnp.float32)
    edge_row = lax.broadcasted_iota(jnp.int32, edges.shape, 1)
    first = lax.broadcasted_iota(jnp.int32, (count, rows, HDIM), 1) == 0
    tensors = []
    for slot, gain_ref in enumerate((query_gain_ref, key_gain_ref, None)):
        part = arrived_ref[:, slot * rows : (slot + 1) * rows, :].astype(jnp.float32)
        own = (edge_row >= slot * SHIFT) & (edge_row < (slot + 1) * SHIFT)
        tail = jnp.sum(jnp.where(own, edges, 0.0), axis=1, keepdims=True)
        before = jnp.concatenate([jnp.zeros_like(tail[:1]), tail[:-1]], axis=0)
        mean = (before + part[:, :1, :]) * (1.0 / SHORT)
        if gain_ref is not None:
            mean = rms_rows(mean) * gain_ref[pl.ds(head, 1), :][None]
        part = jnp.where(first, mean, part).astype(jnp.bfloat16)
        tensors.append(part.reshape(count * rows, HDIM))
    query, key, value = tensors
    diagonal = lax.broadcasted_iota(jnp.int32, (block, block), 1) <= lax.broadcasted_iota(
        jnp.int32, (block, block), 0
    )
    for start in range(0, count * rows, block):
        part = query[start : start + block]
        exponent = masked_exp(across(part, key[start : start + block]), diagonal)
        denominator = jnp.sum(exponent, axis=1, keepdims=True)
        numerator = jnp.dot(
            exponent.astype(jnp.bfloat16),
            value[start : start + block],
            preferred_element_type=jnp.float32,
        )
        if start:
            exponent = masked_exp(across(part, key[:start]), None)
            denominator += jnp.sum(exponent, axis=1, keepdims=True)
            numerator += jnp.dot(
                exponent.astype(jnp.bfloat16), value[:start], preferred_element_type=jnp.float32
            )
        memory_ref[start : start + block, :] = rms_rows(numerator / denominator).astype(
            jnp.bfloat16
        )


def short_attention(arrived, query_gain, key_gain):
    count, depth, _ = arrived.shape
    row_total = count * (depth - EDGE_ROWS) // 3
    return pl.pallas_call(
        functools.partial(short_kernel, math.gcd(128, row_total)),
        out_shape=jax.ShapeDtypeStruct((row_total, HDIM), jnp.bfloat16),
    )(arrived, query_gain.reshape(-1, HDIM), key_gain.reshape(-1, HDIM))


def up_kernel(offsets, up_ref, gain_ref, *refs):
    unit_refs, out_ref = refs[:-1], refs[-1]
    tokens = up_ref.shape[0]
    row_total = unit_refs[0].shape[0]
    device = lax.axis_index("seq")
    limit = device * tokens + lax.broadcasted_iota(jnp.int32, (tokens, row_total), 0)
    visible = SHORT * lax.broadcasted_iota(jnp.int32, (tokens, row_total), 1) <= limit
    for offset, unit_ref in zip(offsets, unit_refs):
        head = device ^ offset
        columns = pl.ds(pl.multiple_of(head * HDIM, HDIM), HDIM)
        query = rms_rows(up_ref[:, columns].astype(jnp.float32)) * gain_ref[pl.ds(head, 1), :]
        memory = unit_ref[...]
        exponent = masked_exp(across(query.astype(jnp.bfloat16), memory), visible)
        denominator = jnp.sum(exponent, axis=1, keepdims=True)
        numerator = jnp.dot(
            exponent.astype(jnp.bfloat16), memory, preferred_element_type=jnp.float32
        )
        out_ref[:, columns] = (numerator / denominator).astype(jnp.bfloat16)


def up_attention(up_query, up_gain, units):
    offsets = tuple(sorted(units))
    return pl.pallas_call(
        functools.partial(up_kernel, offsets),
        out_shape=jax.ShapeDtypeStruct(up_query.shape, jnp.bfloat16),
    )(up_query, up_gain.reshape(-1, HDIM), *[units[offset] for offset in offsets])


def swapped(value, offset):
    count = lax.axis_size("seq")
    return lax.ppermute(value, "seq", [(source, source ^ offset) for source in range(count)])


def memory_gather(query_src, key_src, value_src, up_query, query_gain, key_gain, up_gain):
    outgoing = pool_inputs(query_src, key_src, value_src, query_gain, key_gain, HEADS // 4)
    arrived = lax.all_to_all(outgoing, "seq", split_axis=0, concat_axis=0, tiled=True)
    units = {0: short_attention(arrived, query_gain, key_gain)}
    offset = HEADS // 2
    while offset:
        units.update({held ^ offset: swapped(units[held], offset) for held in list(units)})
        offset //= 2
    return up_attention(up_query, up_gain, units)


def local(*arrays):
    whole = lax.axis_size("seq") == HEADS and HEADS & (HEADS - 1) == 0
    return memory_gather(*arrays) if whole else head_exchange(*arrays)


def solution(mesh):
    in_specs = (
        P(("groups", "seq"), None),
        P(("groups", "seq"), None),
        P(("groups", "seq"), None),
        P(("groups", "seq"), None),
        P(),
        P(),
        P(),
    )
    out_specs = P(("groups", "seq"), None)
    return jax.shard_map(local, mesh=mesh, in_specs=in_specs, out_specs=out_specs, check_vma=False)
```

```python
import functools
import math

import jax
import jax.numpy as jnp
from jax import lax
from jax.experimental import pallas as pl
from jax.experimental.pallas import tpu as pltpu
from jax.sharding import PartitionSpec as P


HEADS = 16
HDIM = 128
SHORT = 4
SHIFT = 3


epsilon = 1e-06


def shifted(value, axis, steps):
    count = lax.axis_size(axis)
    leading, last = (max(0, -steps), min(count, count - steps))
    return lax.ppermute(value, axis, [(source, source + steps) for source in range(leading, last)])


def head_norm(values, gain_vector):
    row_count = values.shape[0]
    by_head = values.reshape(row_count, HEADS, HDIM)
    inverse_rms = lax.rsqrt(jnp.mean(by_head * by_head, axis=2, keepdims=True) + epsilon)
    return (by_head * inverse_rms * gain_vector.reshape(1, HEADS, HDIM)).reshape(
        row_count, HEADS * HDIM
    )


def row_norm(values):
    return values * lax.rsqrt(jnp.mean(values * values, axis=-1, keepdims=True) + epsilon)


def pooled_rows(source, edge_rows):
    widened = jnp.concatenate([edge_rows, source[: source.shape[0] - SHIFT]], axis=0).astype(
        jnp.float32
    )
    return jnp.mean(widened.reshape(-1, SHORT, widened.shape[1]), axis=1)


def blocked_attention(queries, query_limit, key_rows, value_rows, key_positions, block_size):
    head_count, query_count, head_size = queries.shape
    block_total = key_rows.shape[1] // block_size
    ceiling = jnp.max(query_limit)

    def visit_block(block_index, totals):
        offset = block_index * block_size
        block_pos = lax.dynamic_slice_in_dim(key_positions, offset, block_size, 0)

        def compute(state):
            numer_in, denom_in = state
            key_block = lax.dynamic_slice_in_dim(key_rows, offset, block_size, 1)
            value_block = lax.dynamic_slice_in_dim(value_rows, offset, block_size, 1)
            scores = jnp.einsum(
                "hqd,hkd->hqk", queries, key_block, preferred_element_type=jnp.float32
            ) / math.sqrt(HDIM)
            visible = block_pos[None, :] <= query_limit[:, None]
            exponent = jnp.where(visible[None], jnp.exp(scores), 0.0)
            denom_out = denom_in + jnp.sum(exponent, axis=2)
            numer_out = numer_in + jnp.einsum(
                "hqk,hkd->hqd",
                exponent.astype(jnp.bfloat16),
                value_block,
                preferred_element_type=jnp.float32,
            )
            return (numer_out, denom_out)

        return lax.cond(jnp.min(block_pos) <= ceiling, compute, lambda state: state, totals)

    initial = (
        jnp.zeros((head_count, query_count, head_size), jnp.float32),
        jnp.zeros((head_count, query_count), jnp.float32),
    )
    numerator, denominator = lax.fori_loop(0, block_total, visit_block, initial)
    return numerator / denominator[:, :, None]


def spread_heads(matrices, row_count, block_count, device_count):
    count = len(matrices)
    joined = jnp.stack(matrices).reshape(count, row_count, HEADS, HDIM)
    joined = jnp.transpose(joined, (2, 0, 1, 3)).reshape(HEADS, 1, count * row_count, HDIM)
    return jnp.broadcast_to(joined, (HEADS, block_count, count * row_count, HDIM)).reshape(
        device_count, count * row_count, HDIM
    )


def split_pieces(matrix, row_count, block_count, device_count):
    piece = row_count // block_count
    parted = matrix.reshape(block_count, piece, HEADS, HDIM)
    return jnp.transpose(parted, (2, 0, 1, 3)).reshape(device_count, piece, HDIM)


def head_exchange(query_src, key_src, value_src, up_query, query_gain, key_gain, up_gain):
    device_count = lax.axis_size("seq")
    device_index = lax.axis_index("seq")
    block_count = device_count // HEADS
    block_index = device_index % block_count
    token_count = query_src.shape[0]
    edges = jnp.stack(
        [
            query_src[token_count - SHIFT :],
            key_src[token_count - SHIFT :],
            value_src[token_count - SHIFT :],
        ]
    )
    edges = shifted(edges, "seq", 1)
    short_query = head_norm(pooled_rows(query_src, edges[0]), query_gain).astype(jnp.bfloat16)
    short_key = head_norm(pooled_rows(key_src, edges[1]), key_gain).astype(jnp.bfloat16)
    short_value = pooled_rows(value_src, edges[2]).astype(jnp.bfloat16)
    row_count = short_query.shape[0]
    up_heads = head_norm(up_query.astype(jnp.float32), up_gain).astype(jnp.bfloat16)
    row_total = row_count * device_count
    key_block = math.gcd(512, row_total)
    row_positions = jnp.arange(row_total, dtype=jnp.int32)
    device_rows = jnp.arange(device_count, dtype=jnp.int32)[:, None]
    qkv_out = spread_heads(
        [short_query, short_key, short_value], row_count, block_count, device_count
    )
    up_out = split_pieces(up_heads, token_count, block_count, device_count)
    arrived, own_up = (
        lax.all_to_all(qkv_out, "seq", split_axis=0, concat_axis=0, tiled=True),
        lax.all_to_all(up_out, "seq", split_axis=0, concat_axis=0, tiled=True),
    )
    all_query = arrived[:, :row_count].reshape(row_total, HDIM)
    all_key = arrived[:, row_count : 2 * row_count].reshape(row_total, HDIM)
    all_value = arrived[:, 2 * row_count :].reshape(row_total, HDIM)

    def fill_block(index_now, memory_now):
        offset = index_now * key_block
        block_query = lax.dynamic_slice_in_dim(all_query, offset, key_block, 0)[None]
        limits = offset + jnp.arange(key_block, dtype=jnp.int32)
        attended = blocked_attention(
            block_query, limits, all_key[None], all_value[None], row_positions, key_block
        )[0]
        return lax.dynamic_update_slice_in_dim(
            memory_now, row_norm(attended).astype(jnp.bfloat16), offset, 0
        )

    memory = lax.fori_loop(
        0, row_total // key_block, fill_block, jnp.zeros((row_total, HDIM), jnp.bfloat16)
    )
    token_piece = token_count // block_count
    own_tokens = (
        device_rows * token_count
        + block_index * token_piece
        + jnp.arange(token_piece, dtype=jnp.int32)[None, :]
    ).reshape(-1)
    own_up = own_up.reshape(1, device_count * token_piece, HDIM)
    result = blocked_attention(
        own_up, own_tokens // SHORT, memory[None], memory[None], row_positions, key_block
    )[0]
    result = result.astype(jnp.bfloat16).reshape(device_count, token_piece, HDIM)
    returned = lax.all_to_all(result, "seq", split_axis=0, concat_axis=0, tiled=True)
    output_heads = returned.reshape(HEADS, token_count, HDIM)
    return jnp.transpose(output_heads, (1, 0, 2)).reshape(token_count, HEADS * HDIM)


EDGE_ROWS = 16
PEER = 1
CHUNKS = 4


def rms_rows(values):
    return values * lax.rsqrt(jnp.mean(values * values, axis=-1, keepdims=True) + epsilon)


def on_chip(value):
    return pltpu.with_memory_space_constraint(value, pltpu.VMEM)


def select_matrix(tokens, rows, slot):
    row = lax.broadcasted_iota(jnp.int32, (rows + EDGE_ROWS, tokens), 0)
    col = lax.broadcasted_iota(jnp.int32, (rows + EDGE_ROWS, tokens), 1)
    pooled = (row < rows) & (col <= SHORT * row) & (col >= SHORT * row - SHIFT)
    weight = jnp.where(row == 0, 1.0, 1.0 / SHORT)
    edge = (row >= rows + slot * SHIFT) & (row < rows + (slot + 1) * SHIFT)
    edge = edge & (col == tokens - SHIFT + row - rows - slot * SHIFT)
    return jnp.where(pooled, weight, jnp.where(edge, 1.0, 0.0)).astype(jnp.bfloat16)


def pool_kernel(*refs):
    sources, gain_sources, out_ref = refs[:3], refs[3:5], refs[5]
    buffers, gains, source_sems, gain_sems = refs[6:9], refs[9:11], refs[11], refs[12]
    tokens, columns = sources[0].shape
    rows = tokens // SHORT
    width = columns // CHUNKS
    copies = {}
    for chunk in range(CHUNKS):
        part = pl.ds(chunk * width, width)
        for slot in range(3):
            copies[chunk, slot] = pltpu.make_async_copy(
                sources[slot].at[:, part], buffers[slot].at[:, part], source_sems.at[chunk, slot]
            )
            copies[chunk, slot].start()
        if chunk == 0:
            for slot in range(2):
                copies[slot] = pltpu.make_async_copy(
                    gain_sources[slot], gains[slot], gain_sems.at[slot]
                )
                copies[slot].start()
    picks = [select_matrix(tokens, rows, slot) for slot in range(3)]
    first = lax.broadcasted_iota(jnp.int32, (rows, HDIM), 0) == 0
    for chunk in range(CHUNKS):
        picked = []
        for slot in range(3):
            copies[chunk, slot].wait()
            picked.append(
                jnp.dot(
                    picks[slot],
                    buffers[slot][:, chunk * width : (chunk + 1) * width],
                    preferred_element_type=jnp.float32,
                )
            )
        if chunk == 0:
            copies[0].wait()
            copies[1].wait()
        for index in range(width // HDIM):
            head = chunk * (width // HDIM) + index
            inside = slice(index * HDIM, (index + 1) * HDIM)
            for slot in range(3):
                part = picked[slot][:rows, inside]
                if slot < 2:
                    part = jnp.where(first, part, rms_rows(part) * gains[slot][head : head + 1, :])
                out_ref[head, slot * rows : (slot + 1) * rows, :] = part.astype(jnp.bfloat16)
            edge = sum(values[rows:, inside] for values in picked)
            out_ref[head, 3 * rows :, :] = edge.astype(jnp.bfloat16)


def pool_inputs(query_src, key_src, value_src, query_gain, key_gain):
    tokens, columns = query_src.shape
    heads = columns // HDIM
    depth = 3 * (tokens // SHORT) + EDGE_ROWS
    return pl.pallas_call(
        pool_kernel,
        in_specs=[pl.BlockSpec(memory_space=pl.ANY)] * 5,
        out_shape=pltpu.VMEM((heads, depth, HDIM), jnp.bfloat16),
        scratch_shapes=[pltpu.VMEM((tokens, columns), jnp.bfloat16)] * 3
        + [pltpu.VMEM((heads, HDIM), jnp.float32)] * 2
        + [pltpu.SemaphoreType.DMA((CHUNKS, 3)), pltpu.SemaphoreType.DMA((2,))],
    )(query_src, key_src, value_src, query_gain.reshape(heads, HDIM), key_gain.reshape(heads, HDIM))


def masked_exp(scores, visible):
    exponent = jnp.exp(scores * (1.0 / math.sqrt(HDIM)))
    return exponent if visible is None else jnp.where(visible, exponent, 0.0)


def across(left, right):
    return lax.dot_general(
        left, right, (((1,), (1,)), ((), ())), preferred_element_type=jnp.float32
    )


def short_kernel(block, arrived_ref, query_gain_ref, key_gain_ref, memory_ref):
    count, depth, _ = arrived_ref.shape
    rows = (depth - EDGE_ROWS) // 3
    head = lax.axis_index("seq")
    edges = arrived_ref[:, 3 * rows :, :].astype(jnp.float32)
    edge_row = lax.broadcasted_iota(jnp.int32, edges.shape, 1)
    first = lax.broadcasted_iota(jnp.int32, (count, rows, HDIM), 1) == 0
    tensors = []
    for slot, gain_ref in enumerate((query_gain_ref, key_gain_ref, None)):
        part = arrived_ref[:, slot * rows : (slot + 1) * rows, :].astype(jnp.float32)
        own = (edge_row >= slot * SHIFT) & (edge_row < (slot + 1) * SHIFT)
        tail = jnp.sum(jnp.where(own, edges, 0.0), axis=1, keepdims=True)
        before = jnp.concatenate([jnp.zeros_like(tail[:1]), tail[:-1]], axis=0)
        mean = (before + part[:, :1, :]) * (1.0 / SHORT)
        if gain_ref is not None:
            mean = rms_rows(mean) * gain_ref[pl.ds(head, 1), :][None]
        part = jnp.where(first, mean, part).astype(jnp.bfloat16)
        tensors.append(part.reshape(count * rows, HDIM))
    query, key, value = tensors
    diagonal = lax.broadcasted_iota(jnp.int32, (block, block), 1) <= lax.broadcasted_iota(
        jnp.int32, (block, block), 0
    )
    for start in range(0, count * rows, block):
        part = query[start : start + block]
        exponent = masked_exp(across(part, key[start : start + block]), diagonal)
        denominator = jnp.sum(exponent, axis=1, keepdims=True)
        numerator = jnp.dot(
            exponent.astype(jnp.bfloat16),
            value[start : start + block],
            preferred_element_type=jnp.float32,
        )
        if start:
            exponent = masked_exp(across(part, key[:start]), None)
            denominator += jnp.sum(exponent, axis=1, keepdims=True)
            numerator += jnp.dot(
                exponent.astype(jnp.bfloat16), value[:start], preferred_element_type=jnp.float32
            )
        memory_ref[start : start + block, :] = rms_rows(numerator / denominator).astype(
            jnp.bfloat16
        )


def short_attention(arrived, query_gain, key_gain):
    count, depth, _ = arrived.shape
    row_total = count * (depth - EDGE_ROWS) // 3
    return pl.pallas_call(
        functools.partial(short_kernel, math.gcd(128, row_total)),
        out_shape=pltpu.VMEM((row_total, HDIM), jnp.bfloat16),
    )(on_chip(arrived), query_gain.reshape(-1, HDIM), key_gain.reshape(-1, HDIM))


def norm_kernel(up_ref, gain_ref, own_ref, send_ref):
    parity = lax.axis_index("seq") & PEER
    for slot in range(HEADS // 2):
        inside = slice(slot * HDIM, (slot + 1) * HDIM)
        for flip, out_ref in ((0, own_ref), (PEER, send_ref)):
            head = 2 * slot + (parity ^ flip)
            columns = pl.ds(pl.multiple_of(head * HDIM, HDIM), HDIM)
            query = rms_rows(up_ref[:, columns].astype(jnp.float32)) * gain_ref[pl.ds(head, 1), :]
            out_ref[:, inside] = query.astype(jnp.bfloat16)


def norm_up(up_query, up_gain):
    tokens, columns = up_query.shape
    return pl.pallas_call(
        norm_kernel,
        out_shape=[pltpu.VMEM((tokens, columns // 2), jnp.bfloat16)] * 2,
    )(up_query, up_gain.reshape(-1, HDIM))


def up_kernel(offsets, own_ref, peer_ref, *refs):
    unit_refs, own_out_ref, send_out_ref = refs[:-2], refs[-2], refs[-1]
    tokens = own_ref.shape[0]
    row_total = unit_refs[0].shape[0]
    device = lax.axis_index("seq")
    token = lax.broadcasted_iota(jnp.int32, (2 * tokens, row_total), 0)
    first = jnp.where(token < tokens, device * tokens, ((device ^ PEER) - 1) * tokens)
    visible = SHORT * lax.broadcasted_iota(jnp.int32, (2 * tokens, row_total), 1) <= first + token
    for index, (offset, unit_ref) in enumerate(zip(offsets, unit_refs)):
        slot = lax.shift_right_logical(device ^ offset, 1)
        columns = pl.ds(pl.multiple_of(slot * HDIM, HDIM), HDIM)
        query = jnp.concatenate([own_ref[:, columns], peer_ref[:, columns]], axis=0)
        memory = unit_ref[...]
        exponent = masked_exp(across(query, memory), visible)
        denominator = jnp.sum(exponent, axis=1, keepdims=True)
        numerator = jnp.dot(
            exponent.astype(jnp.bfloat16), memory, preferred_element_type=jnp.float32
        )
        result = (numerator / denominator).astype(jnp.bfloat16)
        inside = slice(index * HDIM, (index + 1) * HDIM)
        own_out_ref[:, inside] = result[:tokens]
        send_out_ref[:, inside] = result[tokens:]


def up_attention(own_up, peer_up, units, offsets):
    tokens = own_up.shape[0]
    operands = [own_up, peer_up, *[units[offset] for offset in offsets]]
    return pl.pallas_call(
        functools.partial(up_kernel, offsets),
        out_shape=[pltpu.VMEM((tokens, len(offsets) * HDIM), jnp.bfloat16)] * 2,
    )(*[on_chip(value) for value in operands])


def place_kernel(groups, *refs):
    piece_refs, out_ref = refs[:-1], refs[-1]
    device = lax.axis_index("seq")
    for number, offsets in enumerate(groups):
        for flip in (0, PEER):
            piece_ref = piece_refs[2 * number + flip]
            for index, offset in enumerate(offsets):
                head = device ^ (offset + flip)
                columns = pl.ds(pl.multiple_of(head * HDIM, HDIM), HDIM)
                out_ref[:, columns] = piece_ref[:, index * HDIM : (index + 1) * HDIM]


def place(pieces, groups):
    tokens = pieces[0].shape[0]
    return pl.pallas_call(
        functools.partial(place_kernel, groups),
        out_shape=jax.ShapeDtypeStruct((tokens, HEADS * HDIM), jnp.bfloat16),
    )(*[on_chip(piece) for piece in pieces])


def swapped(value, offset):
    count = lax.axis_size("seq")
    return lax.ppermute(value, "seq", [(source, source ^ offset) for source in range(count)])


def memory_gather(query_src, key_src, value_src, up_query, query_gain, key_gain, up_gain):
    outgoing = pool_inputs(query_src, key_src, value_src, query_gain, key_gain)
    arrived = lax.all_to_all(outgoing, "seq", split_axis=0, concat_axis=0, tiled=True)
    own_up, send_up = norm_up(up_query, up_gain)
    peer_up = swapped(send_up, PEER)
    units = {0: short_attention(arrived, query_gain, key_gain)}
    far = HEADS // 2
    near = tuple(range(2, far, 2))
    units[far] = swapped(units[0], far)
    units.update({offset: swapped(units[0], offset) for offset in near})
    for offset in near:
        units[far + offset] = swapped(units[far], offset)
    groups = ((0,), (*near, far), tuple(far + offset for offset in near))
    pieces = []
    for offsets in groups:
        own, send = up_attention(own_up, peer_up, units, offsets)
        pieces += [own, swapped(send, PEER)]
    return place(pieces, groups)


def local(*arrays):
    whole = lax.axis_size("seq") == HEADS and HEADS & (HEADS - 1) == 0
    return memory_gather(*arrays) if whole else head_exchange(*arrays)


def solution(mesh):
    in_specs = (
        P(("groups", "seq"), None),
        P(("groups", "seq"), None),
        P(("groups", "seq"), None),
        P(("groups", "seq"), None),
        P(),
        P(),
        P(),
    )
    out_specs = P(("groups", "seq"), None)
    return jax.shard_map(local, mesh=mesh, in_specs=in_specs, out_specs=out_specs, check_vma=False)
```

```python
import functools
import math

import jax
import jax.numpy as jnp
from jax import lax
from jax.experimental import pallas as pl
from jax.experimental.pallas import tpu as pltpu
from jax.sharding import PartitionSpec as P


HEADS = 16
HDIM = 128
SHORT = 4
SHIFT = 3


epsilon = 1e-06


def shifted(value, axis, steps):
    count = lax.axis_size(axis)
    leading, last = (max(0, -steps), min(count, count - steps))
    return lax.ppermute(value, axis, [(source, source + steps) for source in range(leading, last)])


def head_norm(values, gain_vector):
    row_count = values.shape[0]
    by_head = values.reshape(row_count, HEADS, HDIM)
    inverse_rms = lax.rsqrt(jnp.mean(by_head * by_head, axis=2, keepdims=True) + epsilon)
    return (by_head * inverse_rms * gain_vector.reshape(1, HEADS, HDIM)).reshape(
        row_count, HEADS * HDIM
    )


def row_norm(values):
    return values * lax.rsqrt(jnp.mean(values * values, axis=-1, keepdims=True) + epsilon)


def pooled_rows(source, edge_rows):
    widened = jnp.concatenate([edge_rows, source[: source.shape[0] - SHIFT]], axis=0).astype(
        jnp.float32
    )
    return jnp.mean(widened.reshape(-1, SHORT, widened.shape[1]), axis=1)


def blocked_attention(queries, query_limit, key_rows, value_rows, key_positions, block_size):
    head_count, query_count, head_size = queries.shape
    block_total = key_rows.shape[1] // block_size
    ceiling = jnp.max(query_limit)

    def visit_block(block_index, totals):
        offset = block_index * block_size
        block_pos = lax.dynamic_slice_in_dim(key_positions, offset, block_size, 0)

        def compute(state):
            numer_in, denom_in = state
            key_block = lax.dynamic_slice_in_dim(key_rows, offset, block_size, 1)
            value_block = lax.dynamic_slice_in_dim(value_rows, offset, block_size, 1)
            scores = jnp.einsum(
                "hqd,hkd->hqk", queries, key_block, preferred_element_type=jnp.float32
            ) / math.sqrt(HDIM)
            visible = block_pos[None, :] <= query_limit[:, None]
            exponent = jnp.where(visible[None], jnp.exp(scores), 0.0)
            denom_out = denom_in + jnp.sum(exponent, axis=2)
            numer_out = numer_in + jnp.einsum(
                "hqk,hkd->hqd",
                exponent.astype(jnp.bfloat16),
                value_block,
                preferred_element_type=jnp.float32,
            )
            return (numer_out, denom_out)

        return lax.cond(jnp.min(block_pos) <= ceiling, compute, lambda state: state, totals)

    initial = (
        jnp.zeros((head_count, query_count, head_size), jnp.float32),
        jnp.zeros((head_count, query_count), jnp.float32),
    )
    numerator, denominator = lax.fori_loop(0, block_total, visit_block, initial)
    return numerator / denominator[:, :, None]


def spread_heads(matrices, row_count, block_count, device_count):
    count = len(matrices)
    joined = jnp.stack(matrices).reshape(count, row_count, HEADS, HDIM)
    joined = jnp.transpose(joined, (2, 0, 1, 3)).reshape(HEADS, 1, count * row_count, HDIM)
    return jnp.broadcast_to(joined, (HEADS, block_count, count * row_count, HDIM)).reshape(
        device_count, count * row_count, HDIM
    )


def split_pieces(matrix, row_count, block_count, device_count):
    piece = row_count // block_count
    parted = matrix.reshape(block_count, piece, HEADS, HDIM)
    return jnp.transpose(parted, (2, 0, 1, 3)).reshape(device_count, piece, HDIM)


def head_exchange(query_src, key_src, value_src, up_query, query_gain, key_gain, up_gain):
    device_count = lax.axis_size("seq")
    device_index = lax.axis_index("seq")
    block_count = device_count // HEADS
    block_index = device_index % block_count
    token_count = query_src.shape[0]
    edges = jnp.stack(
        [
            query_src[token_count - SHIFT :],
            key_src[token_count - SHIFT :],
            value_src[token_count - SHIFT :],
        ]
    )
    edges = shifted(edges, "seq", 1)
    short_query = head_norm(pooled_rows(query_src, edges[0]), query_gain).astype(jnp.bfloat16)
    short_key = head_norm(pooled_rows(key_src, edges[1]), key_gain).astype(jnp.bfloat16)
    short_value = pooled_rows(value_src, edges[2]).astype(jnp.bfloat16)
    row_count = short_query.shape[0]
    up_heads = head_norm(up_query.astype(jnp.float32), up_gain).astype(jnp.bfloat16)
    row_total = row_count * device_count
    key_block = math.gcd(512, row_total)
    row_positions = jnp.arange(row_total, dtype=jnp.int32)
    device_rows = jnp.arange(device_count, dtype=jnp.int32)[:, None]
    qkv_out = spread_heads(
        [short_query, short_key, short_value], row_count, block_count, device_count
    )
    up_out = split_pieces(up_heads, token_count, block_count, device_count)
    arrived, own_up = (
        lax.all_to_all(qkv_out, "seq", split_axis=0, concat_axis=0, tiled=True),
        lax.all_to_all(up_out, "seq", split_axis=0, concat_axis=0, tiled=True),
    )
    all_query = arrived[:, :row_count].reshape(row_total, HDIM)
    all_key = arrived[:, row_count : 2 * row_count].reshape(row_total, HDIM)
    all_value = arrived[:, 2 * row_count :].reshape(row_total, HDIM)

    def fill_block(index_now, memory_now):
        offset = index_now * key_block
        block_query = lax.dynamic_slice_in_dim(all_query, offset, key_block, 0)[None]
        limits = offset + jnp.arange(key_block, dtype=jnp.int32)
        attended = blocked_attention(
            block_query, limits, all_key[None], all_value[None], row_positions, key_block
        )[0]
        return lax.dynamic_update_slice_in_dim(
            memory_now, row_norm(attended).astype(jnp.bfloat16), offset, 0
        )

    memory = lax.fori_loop(
        0, row_total // key_block, fill_block, jnp.zeros((row_total, HDIM), jnp.bfloat16)
    )
    token_piece = token_count // block_count
    own_tokens = (
        device_rows * token_count
        + block_index * token_piece
        + jnp.arange(token_piece, dtype=jnp.int32)[None, :]
    ).reshape(-1)
    own_up = own_up.reshape(1, device_count * token_piece, HDIM)
    result = blocked_attention(
        own_up, own_tokens // SHORT, memory[None], memory[None], row_positions, key_block
    )[0]
    result = result.astype(jnp.bfloat16).reshape(device_count, token_piece, HDIM)
    returned = lax.all_to_all(result, "seq", split_axis=0, concat_axis=0, tiled=True)
    output_heads = returned.reshape(HEADS, token_count, HDIM)
    return jnp.transpose(output_heads, (1, 0, 2)).reshape(token_count, HEADS * HDIM)


EDGE_ROWS = 16
PEER = 1
CHUNKS = 4


def rms_rows(values):
    return values * lax.rsqrt(jnp.mean(values * values, axis=-1, keepdims=True) + epsilon)


def on_chip(value):
    return pltpu.with_memory_space_constraint(value, pltpu.VMEM)


def select_matrix(tokens, rows, slot):
    row = lax.broadcasted_iota(jnp.int32, (rows + EDGE_ROWS, tokens), 0)
    col = lax.broadcasted_iota(jnp.int32, (rows + EDGE_ROWS, tokens), 1)
    pooled = (row < rows) & (col <= SHORT * row) & (col >= SHORT * row - SHIFT)
    weight = jnp.where(row == 0, 1.0, 1.0 / SHORT)
    edge = (row >= rows + slot * SHIFT) & (row < rows + (slot + 1) * SHIFT)
    edge = edge & (col == tokens - SHIFT + row - rows - slot * SHIFT)
    return jnp.where(pooled, weight, jnp.where(edge, 1.0, 0.0)).astype(jnp.bfloat16)


def pool_kernel(*refs):
    sources, gain_sources, out_ref = refs[:3], refs[3:5], refs[5]
    buffers, gains, source_sems, gain_sems = refs[6:9], refs[9:11], refs[11], refs[12]
    tokens, columns = sources[0].shape
    rows = tokens // SHORT
    width = columns // CHUNKS
    copies = {}
    for chunk in range(CHUNKS):
        part = pl.ds(chunk * width, width)
        for slot in range(3):
            copies[chunk, slot] = pltpu.make_async_copy(
                sources[slot].at[:, part], buffers[slot].at[:, part], source_sems.at[chunk, slot]
            )
            copies[chunk, slot].start()
        if chunk == 0:
            for slot in range(2):
                copies[slot] = pltpu.make_async_copy(
                    gain_sources[slot], gains[slot], gain_sems.at[slot]
                )
                copies[slot].start()
    picks = [select_matrix(tokens, rows, slot) for slot in range(3)]
    first = lax.broadcasted_iota(jnp.int32, (rows, HDIM), 0) == 0
    for chunk in range(CHUNKS):
        picked = []
        for slot in range(3):
            copies[chunk, slot].wait()
            picked.append(
                jnp.dot(
                    picks[slot],
                    buffers[slot][:, chunk * width : (chunk + 1) * width],
                    preferred_element_type=jnp.float32,
                )
            )
        if chunk == 0:
            copies[0].wait()
            copies[1].wait()
        for index in range(width // HDIM):
            head = chunk * (width // HDIM) + index
            inside = slice(index * HDIM, (index + 1) * HDIM)
            for slot in range(3):
                part = picked[slot][:rows, inside]
                if slot < 2:
                    part = jnp.where(first, part, rms_rows(part) * gains[slot][head : head + 1, :])
                out_ref[head, slot * rows : (slot + 1) * rows, :] = part.astype(jnp.bfloat16)
            edge = sum(values[rows:, inside] for values in picked)
            out_ref[head, 3 * rows :, :] = edge.astype(jnp.bfloat16)


def pool_inputs(query_src, key_src, value_src, query_gain, key_gain):
    tokens, columns = query_src.shape
    heads = columns // HDIM
    depth = 3 * (tokens // SHORT) + EDGE_ROWS
    return pl.pallas_call(
        pool_kernel,
        in_specs=[pl.BlockSpec(memory_space=pl.ANY)] * 5,
        out_shape=pltpu.VMEM((heads, depth, HDIM), jnp.bfloat16),
        scratch_shapes=[pltpu.VMEM((tokens, columns), jnp.bfloat16)] * 3
        + [pltpu.VMEM((heads, HDIM), jnp.float32)] * 2
        + [pltpu.SemaphoreType.DMA((CHUNKS, 3)), pltpu.SemaphoreType.DMA((2,))],
    )(query_src, key_src, value_src, query_gain.reshape(heads, HDIM), key_gain.reshape(heads, HDIM))


def masked_exp(scores, visible):
    exponent = jnp.exp(scores * (1.0 / math.sqrt(HDIM)))
    return exponent if visible is None else jnp.where(visible, exponent, 0.0)


def across(left, right):
    return lax.dot_general(
        left, right, (((1,), (1,)), ((), ())), preferred_element_type=jnp.float32
    )


def short_kernel(block, arrived_ref, query_gain_ref, key_gain_ref, memory_ref):
    count, depth, _ = arrived_ref.shape
    rows = (depth - EDGE_ROWS) // 3
    head = lax.axis_index("seq")
    edges = arrived_ref[:, 3 * rows :, :].astype(jnp.float32)
    edge_row = lax.broadcasted_iota(jnp.int32, edges.shape, 1)
    first = lax.broadcasted_iota(jnp.int32, (count, rows, HDIM), 1) == 0
    tensors = []
    for slot, gain_ref in enumerate((query_gain_ref, key_gain_ref, None)):
        part = arrived_ref[:, slot * rows : (slot + 1) * rows, :].astype(jnp.float32)
        own = (edge_row >= slot * SHIFT) & (edge_row < (slot + 1) * SHIFT)
        tail = jnp.sum(jnp.where(own, edges, 0.0), axis=1, keepdims=True)
        before = jnp.concatenate([jnp.zeros_like(tail[:1]), tail[:-1]], axis=0)
        mean = (before + part[:, :1, :]) * (1.0 / SHORT)
        if gain_ref is not None:
            mean = rms_rows(mean) * gain_ref[pl.ds(head, 1), :][None]
        part = jnp.where(first, mean, part).astype(jnp.bfloat16)
        tensors.append(part.reshape(count * rows, HDIM))
    query, key, value = tensors
    diagonal = lax.broadcasted_iota(jnp.int32, (block, block), 1) <= lax.broadcasted_iota(
        jnp.int32, (block, block), 0
    )
    for start in range(0, count * rows, block):
        part = query[start : start + block]
        exponent = masked_exp(across(part, key[start : start + block]), diagonal)
        denominator = jnp.sum(exponent, axis=1, keepdims=True)
        numerator = jnp.dot(
            exponent.astype(jnp.bfloat16),
            value[start : start + block],
            preferred_element_type=jnp.float32,
        )
        if start:
            exponent = masked_exp(across(part, key[:start]), None)
            denominator += jnp.sum(exponent, axis=1, keepdims=True)
            numerator += jnp.dot(
                exponent.astype(jnp.bfloat16), value[:start], preferred_element_type=jnp.float32
            )
        memory_ref[start : start + block, :] = rms_rows(numerator / denominator).astype(
            jnp.bfloat16
        )


def short_attention(arrived, query_gain, key_gain):
    count, depth, _ = arrived.shape
    row_total = count * (depth - EDGE_ROWS) // 3
    return pl.pallas_call(
        functools.partial(short_kernel, math.gcd(128, row_total)),
        out_shape=pltpu.VMEM((row_total, HDIM), jnp.bfloat16),
    )(on_chip(arrived), query_gain.reshape(-1, HDIM), key_gain.reshape(-1, HDIM))


def norm_kernel(up_ref, gain_ref, own_ref, send_ref):
    parity = lax.axis_index("seq") & PEER
    for slot in range(HEADS // 2):
        inside = slice(slot * HDIM, (slot + 1) * HDIM)
        for flip, out_ref in ((0, own_ref), (PEER, send_ref)):
            head = 2 * slot + (parity ^ flip)
            columns = pl.ds(pl.multiple_of(head * HDIM, HDIM), HDIM)
            query = rms_rows(up_ref[:, columns].astype(jnp.float32)) * gain_ref[pl.ds(head, 1), :]
            out_ref[:, inside] = query.astype(jnp.bfloat16)


def norm_up(up_query, up_gain):
    tokens, columns = up_query.shape
    return pl.pallas_call(
        norm_kernel,
        out_shape=[pltpu.VMEM((tokens, columns // 2), jnp.bfloat16)] * 2,
    )(up_query, up_gain.reshape(-1, HDIM))


def pick_kernel(far, nears, own_ref, peer_ref, *out_refs):
    tokens = own_ref.shape[0]
    device = lax.axis_index("seq")
    for near, out_ref in zip(nears, out_refs):
        for kind in range(2):
            slot = lax.shift_right_logical(device ^ (near + kind * far), 1)
            columns = pl.ds(pl.multiple_of(slot * HDIM, HDIM), HDIM)
            out_ref[kind, :tokens, :] = own_ref[:, columns]
            out_ref[kind, tokens:, :] = peer_ref[:, columns]


def pick_up(own_up, peer_up, far, nears):
    tokens = own_up.shape[0]
    return pl.pallas_call(
        functools.partial(pick_kernel, far, nears),
        out_shape=[pltpu.VMEM((2, 2 * tokens, HDIM), jnp.bfloat16)] * len(nears),
    )(on_chip(own_up), on_chip(peer_up))


def attend_kernel(kind, nears, memory_ref, *refs):
    query_refs, out_refs = refs[: len(nears)], refs[len(nears) :]
    double = query_refs[0].shape[1]
    tokens = double // 2
    row_total = memory_ref.shape[0]
    device = lax.axis_index("seq")
    memory = memory_ref[...]
    token = lax.broadcasted_iota(jnp.int32, (double, row_total), 0)
    column = SHORT * lax.broadcasted_iota(jnp.int32, (double, row_total), 1)
    for near, query_ref, out_ref in zip(nears, query_refs, out_refs):
        source = device ^ near
        first = jnp.where(token < tokens, source * tokens, ((source ^ PEER) - 1) * tokens)
        exponent = masked_exp(across(query_ref[kind], memory), column <= first + token)
        denominator = jnp.sum(exponent, axis=1, keepdims=True)
        numerator = jnp.dot(
            exponent.astype(jnp.bfloat16), memory, preferred_element_type=jnp.float32
        )
        out_ref[...] = (numerator / denominator).astype(jnp.bfloat16)


def attend(kind, nears, memory, queries):
    double = queries[nears[0]].shape[1]
    operands = [memory, *[queries[near] for near in nears]]
    results = pl.pallas_call(
        functools.partial(attend_kernel, kind, nears),
        out_shape=[pltpu.VMEM((double, HDIM), jnp.bfloat16)] * len(nears),
    )(*[on_chip(value) for value in operands])
    return dict(zip(nears, results))


def pack_kernel(*refs):
    piece_refs, out_ref = refs[:-1], refs[-1]
    tokens = out_ref.shape[0]
    for index, piece_ref in enumerate(piece_refs):
        out_ref[:, index * HDIM : (index + 1) * HDIM] = piece_ref[tokens:, :]


def pack(pieces):
    tokens = pieces[0].shape[0] // 2
    return pl.pallas_call(
        pack_kernel,
        out_shape=pltpu.VMEM((tokens, len(pieces) * HDIM), jnp.bfloat16),
    )(*[on_chip(piece) for piece in pieces])


def place_kernel(offsets, *refs):
    piece_refs, peer_ref, out_ref = refs[:-2], refs[-2], refs[-1]
    tokens = out_ref.shape[0]
    device = lax.axis_index("seq")
    for index, (offset, piece_ref) in enumerate(zip(offsets, piece_refs)):
        for flip in (0, PEER):
            head = device ^ (offset + flip)
            columns = pl.ds(pl.multiple_of(head * HDIM, HDIM), HDIM)
            if flip:
                out_ref[:, columns] = peer_ref[:, index * HDIM : (index + 1) * HDIM]
            else:
                out_ref[:, columns] = piece_ref[:tokens, :]


def place(offsets, pieces, peer):
    return pl.pallas_call(
        functools.partial(place_kernel, offsets),
        out_shape=jax.ShapeDtypeStruct((peer.shape[0], HEADS * HDIM), jnp.bfloat16),
    )(*[on_chip(piece) for piece in pieces], on_chip(peer))


def swapped(value, offset):
    count = lax.axis_size("seq")
    return lax.ppermute(value, "seq", [(source, source ^ offset) for source in range(count)])


def half_exchange(query_src, key_src, value_src, up_query, query_gain, key_gain, up_gain):
    far = HEADS // 2
    nears = tuple(range(0, far, 2))
    outgoing = pool_inputs(query_src, key_src, value_src, query_gain, key_gain)
    arrived = lax.all_to_all(outgoing, "seq", split_axis=0, concat_axis=0, tiled=True)
    own_up, send_up = norm_up(up_query, up_gain)
    peer_up = swapped(send_up, PEER)
    queries = dict(zip(nears, pick_up(own_up, peer_up, far, nears)))
    for near in nears[1:]:
        queries[near] = swapped(queries[near], near)
    memory = short_attention(arrived, query_gain, key_gain)
    far_memory = swapped(memory, far)
    offsets, pieces = [], []
    for kind, held in enumerate((memory, far_memory)):
        results = attend(kind, nears, held, queries)
        for near in nears:
            pieces.append(swapped(results[near], near) if near else results[near])
            offsets.append(near + kind * far)
    packed = pack(pieces)
    peer = swapped(packed, PEER)
    return place(tuple(offsets), pieces, peer)


def local(*arrays):
    whole = lax.axis_size("seq") == HEADS and HEADS & (HEADS - 1) == 0
    return half_exchange(*arrays) if whole else head_exchange(*arrays)


def solution(mesh):
    in_specs = (
        P(("groups", "seq"), None),
        P(("groups", "seq"), None),
        P(("groups", "seq"), None),
        P(("groups", "seq"), None),
        P(),
        P(),
        P(),
    )
    out_specs = P(("groups", "seq"), None)
    return jax.shard_map(local, mesh=mesh, in_specs=in_specs, out_specs=out_specs, check_vma=False)
```

```python
import functools
import math

import jax
import jax.numpy as jnp
from jax import lax
from jax.experimental import pallas as pl
from jax.experimental.pallas import tpu as pltpu
from jax.sharding import PartitionSpec as P


HEADS = 16
HDIM = 128
SHORT = 4
SHIFT = 3


epsilon = 1e-06


def shifted(value, axis, steps):
    count = lax.axis_size(axis)
    leading, last = (max(0, -steps), min(count, count - steps))
    return lax.ppermute(value, axis, [(source, source + steps) for source in range(leading, last)])


def head_norm(values, gain_vector):
    row_count = values.shape[0]
    by_head = values.reshape(row_count, HEADS, HDIM)
    inverse_rms = lax.rsqrt(jnp.mean(by_head * by_head, axis=2, keepdims=True) + epsilon)
    return (by_head * inverse_rms * gain_vector.reshape(1, HEADS, HDIM)).reshape(
        row_count, HEADS * HDIM
    )


def row_norm(values):
    return values * lax.rsqrt(jnp.mean(values * values, axis=-1, keepdims=True) + epsilon)


def pooled_rows(source, edge_rows):
    widened = jnp.concatenate([edge_rows, source[: source.shape[0] - SHIFT]], axis=0).astype(
        jnp.float32
    )
    return jnp.mean(widened.reshape(-1, SHORT, widened.shape[1]), axis=1)


def blocked_attention(queries, query_limit, key_rows, value_rows, key_positions, block_size):
    head_count, query_count, head_size = queries.shape
    block_total = key_rows.shape[1] // block_size
    ceiling = jnp.max(query_limit)

    def visit_block(block_index, totals):
        offset = block_index * block_size
        block_pos = lax.dynamic_slice_in_dim(key_positions, offset, block_size, 0)

        def compute(state):
            numer_in, denom_in = state
            key_block = lax.dynamic_slice_in_dim(key_rows, offset, block_size, 1)
            value_block = lax.dynamic_slice_in_dim(value_rows, offset, block_size, 1)
            scores = jnp.einsum(
                "hqd,hkd->hqk", queries, key_block, preferred_element_type=jnp.float32
            ) / math.sqrt(HDIM)
            visible = block_pos[None, :] <= query_limit[:, None]
            exponent = jnp.where(visible[None], jnp.exp(scores), 0.0)
            denom_out = denom_in + jnp.sum(exponent, axis=2)
            numer_out = numer_in + jnp.einsum(
                "hqk,hkd->hqd",
                exponent.astype(jnp.bfloat16),
                value_block,
                preferred_element_type=jnp.float32,
            )
            return (numer_out, denom_out)

        return lax.cond(jnp.min(block_pos) <= ceiling, compute, lambda state: state, totals)

    initial = (
        jnp.zeros((head_count, query_count, head_size), jnp.float32),
        jnp.zeros((head_count, query_count), jnp.float32),
    )
    numerator, denominator = lax.fori_loop(0, block_total, visit_block, initial)
    return numerator / denominator[:, :, None]


def spread_heads(matrices, row_count, block_count, device_count):
    count = len(matrices)
    joined = jnp.stack(matrices).reshape(count, row_count, HEADS, HDIM)
    joined = jnp.transpose(joined, (2, 0, 1, 3)).reshape(HEADS, 1, count * row_count, HDIM)
    return jnp.broadcast_to(joined, (HEADS, block_count, count * row_count, HDIM)).reshape(
        device_count, count * row_count, HDIM
    )


def split_pieces(matrix, row_count, block_count, device_count):
    piece = row_count // block_count
    parted = matrix.reshape(block_count, piece, HEADS, HDIM)
    return jnp.transpose(parted, (2, 0, 1, 3)).reshape(device_count, piece, HDIM)


def head_exchange(query_src, key_src, value_src, up_query, query_gain, key_gain, up_gain):
    device_count = lax.axis_size("seq")
    device_index = lax.axis_index("seq")
    block_count = device_count // HEADS
    block_index = device_index % block_count
    token_count = query_src.shape[0]
    edges = jnp.stack(
        [
            query_src[token_count - SHIFT :],
            key_src[token_count - SHIFT :],
            value_src[token_count - SHIFT :],
        ]
    )
    edges = shifted(edges, "seq", 1)
    short_query = head_norm(pooled_rows(query_src, edges[0]), query_gain).astype(jnp.bfloat16)
    short_key = head_norm(pooled_rows(key_src, edges[1]), key_gain).astype(jnp.bfloat16)
    short_value = pooled_rows(value_src, edges[2]).astype(jnp.bfloat16)
    row_count = short_query.shape[0]
    up_heads = head_norm(up_query.astype(jnp.float32), up_gain).astype(jnp.bfloat16)
    row_total = row_count * device_count
    key_block = math.gcd(512, row_total)
    row_positions = jnp.arange(row_total, dtype=jnp.int32)
    device_rows = jnp.arange(device_count, dtype=jnp.int32)[:, None]
    qkv_out = spread_heads(
        [short_query, short_key, short_value], row_count, block_count, device_count
    )
    up_out = split_pieces(up_heads, token_count, block_count, device_count)
    arrived, own_up = (
        lax.all_to_all(qkv_out, "seq", split_axis=0, concat_axis=0, tiled=True),
        lax.all_to_all(up_out, "seq", split_axis=0, concat_axis=0, tiled=True),
    )
    all_query = arrived[:, :row_count].reshape(row_total, HDIM)
    all_key = arrived[:, row_count : 2 * row_count].reshape(row_total, HDIM)
    all_value = arrived[:, 2 * row_count :].reshape(row_total, HDIM)

    def fill_block(index_now, memory_now):
        offset = index_now * key_block
        block_query = lax.dynamic_slice_in_dim(all_query, offset, key_block, 0)[None]
        limits = offset + jnp.arange(key_block, dtype=jnp.int32)
        attended = blocked_attention(
            block_query, limits, all_key[None], all_value[None], row_positions, key_block
        )[0]
        return lax.dynamic_update_slice_in_dim(
            memory_now, row_norm(attended).astype(jnp.bfloat16), offset, 0
        )

    memory = lax.fori_loop(
        0, row_total // key_block, fill_block, jnp.zeros((row_total, HDIM), jnp.bfloat16)
    )
    token_piece = token_count // block_count
    own_tokens = (
        device_rows * token_count
        + block_index * token_piece
        + jnp.arange(token_piece, dtype=jnp.int32)[None, :]
    ).reshape(-1)
    own_up = own_up.reshape(1, device_count * token_piece, HDIM)
    result = blocked_attention(
        own_up, own_tokens // SHORT, memory[None], memory[None], row_positions, key_block
    )[0]
    result = result.astype(jnp.bfloat16).reshape(device_count, token_piece, HDIM)
    returned = lax.all_to_all(result, "seq", split_axis=0, concat_axis=0, tiled=True)
    output_heads = returned.reshape(HEADS, token_count, HDIM)
    return jnp.transpose(output_heads, (1, 0, 2)).reshape(token_count, HEADS * HDIM)


EDGE_ROWS = 16
PEER = 1


def rms_rows(values):
    return values * lax.rsqrt(jnp.mean(values * values, axis=-1, keepdims=True) + epsilon)


def on_chip(value):
    return pltpu.with_memory_space_constraint(value, pltpu.VMEM)


def select_matrix(tokens, rows, slot):
    row = lax.broadcasted_iota(jnp.int32, (rows + EDGE_ROWS, tokens), 0)
    col = lax.broadcasted_iota(jnp.int32, (rows + EDGE_ROWS, tokens), 1)
    pooled = (row < rows) & (col <= SHORT * row) & (col >= SHORT * row - SHIFT)
    weight = jnp.where(row == 0, 1.0, 1.0 / SHORT)
    edge = (row >= rows + slot * SHIFT) & (row < rows + (slot + 1) * SHIFT)
    edge = edge & (col == tokens - SHIFT + row - rows - slot * SHIFT)
    return jnp.where(pooled, weight, jnp.where(edge, 1.0, 0.0)).astype(jnp.bfloat16)


def pool_kernel(*refs):
    sources, out_hbm = refs[:5], refs[5]
    buffers, out_ref, in_sems, out_sems = refs[6:11], refs[11], refs[12], refs[13]
    tokens, columns = sources[0].shape
    rows = tokens // SHORT
    copies = [
        pltpu.make_async_copy(source, buffer, in_sems.at[index])
        for index, (source, buffer) in enumerate(zip(sources, buffers))
    ]
    for index in (0, 3, 1, 4, 2):
        copies[index].start()
    picks = [select_matrix(tokens, rows, slot) for slot in range(3)]
    first = lax.broadcasted_iota(jnp.int32, (rows, HDIM), 0) == 0
    edges, returns = [], []
    for slot in range(3):
        copies[slot].wait()
        if slot < 2:
            copies[3 + slot].wait()
        picked = jnp.dot(picks[slot], buffers[slot][...], preferred_element_type=jnp.float32)
        edges.append(picked[rows:])
        span = rows if slot < 2 else rows + EDGE_ROWS
        for head in range(columns // HDIM):
            inside = slice(head * HDIM, (head + 1) * HDIM)
            part = picked[:rows, inside]
            if slot < 2:
                gain = buffers[3 + slot][head : head + 1, :]
                part = jnp.where(first, part, rms_rows(part) * gain)
            else:
                edge = sum(values[:, inside] for values in edges)
                out_ref[head, 3 * rows :, :] = edge.astype(jnp.bfloat16)
            out_ref[head, slot * rows : (slot + 1) * rows, :] = part.astype(jnp.bfloat16)
        target = pl.ds(slot * rows, span)
        copy = pltpu.make_async_copy(
            out_ref.at[:, target], out_hbm.at[:, target], out_sems.at[slot]
        )
        copy.start()
        returns.append(copy)
    for copy in returns:
        copy.wait()


def pool_inputs(query_src, key_src, value_src, query_gain, key_gain):
    tokens, columns = query_src.shape
    heads = columns // HDIM
    depth = 3 * (tokens // SHORT) + EDGE_ROWS
    return pl.pallas_call(
        pool_kernel,
        in_specs=[pl.BlockSpec(memory_space=pl.ANY)] * 5,
        out_specs=pl.BlockSpec(memory_space=pl.ANY),
        out_shape=jax.ShapeDtypeStruct((heads, depth, HDIM), jnp.bfloat16),
        scratch_shapes=[pltpu.VMEM((tokens, columns), jnp.bfloat16)] * 3
        + [pltpu.VMEM((heads, HDIM), jnp.float32)] * 2
        + [pltpu.VMEM((heads, depth, HDIM), jnp.bfloat16)]
        + [pltpu.SemaphoreType.DMA((5,)), pltpu.SemaphoreType.DMA((3,))],
    )(query_src, key_src, value_src, query_gain.reshape(heads, HDIM), key_gain.reshape(heads, HDIM))


def scaled_exp(scores):
    return jnp.exp2(scores * (math.log2(math.e) / math.sqrt(HDIM)))


def across(left, right):
    return lax.dot_general(
        left, right, (((1,), (1,)), ((), ())), preferred_element_type=jnp.float32
    )


def short_kernel(block, arrived_ref, query_gain_ref, key_gain_ref, memory_ref):
    count, depth, _ = arrived_ref.shape
    rows = (depth - EDGE_ROWS) // 3
    total = count * rows
    head = lax.axis_index("seq")
    edges = arrived_ref[:, 3 * rows :, :].astype(jnp.float32)
    edge_row = lax.broadcasted_iota(jnp.int32, edges.shape, 1)
    first = lax.broadcasted_iota(jnp.int32, (count, rows, HDIM), 1) == 0
    tensors = []
    for slot, gain_ref in enumerate((query_gain_ref, key_gain_ref, None)):
        part = arrived_ref[:, slot * rows : (slot + 1) * rows, :].astype(jnp.float32)
        own = (edge_row >= slot * SHIFT) & (edge_row < (slot + 1) * SHIFT)
        tail = jnp.sum(jnp.where(own, edges, 0.0), axis=1, keepdims=True)
        before = jnp.concatenate([jnp.zeros_like(tail[:1]), tail[:-1]], axis=0)
        mean = (before + part[:, :1, :]) * (1.0 / SHORT)
        if gain_ref is not None:
            mean = rms_rows(mean) * gain_ref[pl.ds(head, 1), :][None]
        part = jnp.where(first, mean, part).astype(jnp.bfloat16)
        tensors.append(part.reshape(total, HDIM))
    query, key, value = tensors
    diagonal = lax.broadcasted_iota(jnp.int32, (block, block), 1) <= lax.broadcasted_iota(
        jnp.int32, (block, block), 0
    )
    starts = range(0, total, block)
    sums = [0.0] * len(starts)
    numerators = [0.0] * len(starts)
    for index, start in enumerate(starts):
        exponent = scaled_exp(across(query[start:], key[start : start + block]))
        for later in range(index, len(starts)):
            offset = (later - index) * block
            part = exponent[offset : offset + block]
            if later == index:
                part = jnp.where(diagonal, part, 0.0)
            sums[later] += part
            numerators[later] += jnp.dot(
                part.astype(jnp.bfloat16),
                value[start : start + block],
                preferred_element_type=jnp.float32,
            )
    for index, start in enumerate(starts):
        denominator = jnp.sum(sums[index], axis=1, keepdims=True)
        memory_ref[start : start + block, :] = rms_rows(numerators[index] / denominator).astype(
            jnp.bfloat16
        )


def short_attention(arrived, query_gain, key_gain):
    count, depth, _ = arrived.shape
    row_total = count * (depth - EDGE_ROWS) // 3
    return pl.pallas_call(
        functools.partial(short_kernel, math.gcd(128, row_total)),
        out_shape=pltpu.VMEM((row_total, HDIM), jnp.bfloat16),
    )(on_chip(arrived), query_gain.reshape(-1, HDIM), key_gain.reshape(-1, HDIM))


def norm_kernel(shifts, nears, up_ref, gain_ref, *out_refs):
    device = lax.axis_index("seq")
    for near, out_ref in zip(nears, out_refs):
        for index, shift in enumerate(shifts):
            head = device ^ (near + shift)
            columns = pl.ds(pl.multiple_of(head * HDIM, HDIM), HDIM)
            query = rms_rows(up_ref[:, columns].astype(jnp.float32)) * gain_ref[pl.ds(head, 1), :]
            out_ref[index] = query.astype(jnp.bfloat16)


def norm_up(up_query, up_gain, shifts, nears):
    tokens = up_query.shape[0]
    shape = pltpu.VMEM((len(shifts), tokens, HDIM), jnp.bfloat16)
    return pl.pallas_call(
        functools.partial(norm_kernel, shifts, nears), out_shape=[shape] * len(nears)
    )(up_query, up_gain.reshape(-1, HDIM))


def attend_kernel(nears, first, held, *refs):
    count = len(nears)
    memory_refs, refs = refs[: len(held)], refs[len(held) :]
    query_refs, out_refs = refs[:count], refs[-count:]
    done_refs = refs[count:-count]
    tokens = query_refs[0].shape[1]
    row_total = memory_refs[0].shape[0]
    device = lax.axis_index("seq")
    token = lax.broadcasted_iota(jnp.int32, (tokens, row_total), 0)
    column = SHORT * lax.broadcasted_iota(jnp.int32, (tokens, row_total), 1)
    for order in range(count):
        if first:
            out_refs[order][:first] = done_refs[order][...]
        visible = column - token <= (device ^ nears[order]) * tokens
        for index, (memory_ref, slot) in enumerate(zip(memory_refs, held)):
            memory = memory_ref[...]
            exponent = scaled_exp(across(query_refs[order][slot], memory))
            exponent = jnp.where(visible, exponent, 0.0)
            denominator = jnp.sum(exponent, axis=1, keepdims=True)
            numerator = jnp.dot(
                exponent.astype(jnp.bfloat16), memory, preferred_element_type=jnp.float32
            )
            out_refs[order][first + index] = (numerator / denominator).astype(jnp.bfloat16)


def attend(nears, memories, held, queries, done):
    tokens = queries[nears[0]].shape[1]
    first = done[nears[0]].shape[0] if done else 0
    operands = [*memories, *[queries[near] for near in nears]]
    operands += [done[near] for near in nears] if done else []
    shape = pltpu.VMEM((first + len(held), tokens, HDIM), jnp.bfloat16)
    results = pl.pallas_call(
        functools.partial(attend_kernel, nears, first, held), out_shape=[shape] * len(nears)
    )(*[on_chip(value) for value in operands])
    return dict(zip(nears, results))


def place_kernel(offsets, *refs):
    piece_refs, out_hbm, sems = refs[:-2], refs[-2], refs[-1]
    device = lax.axis_index("seq")
    copies = []
    for number, (offset, piece_ref) in enumerate(zip(offsets, piece_refs)):
        for flip in (0, PEER):
            head = device ^ (offset + flip)
            columns = pl.ds(pl.multiple_of(head * HDIM, HDIM), HDIM)
            copy = pltpu.make_async_copy(
                piece_ref.at[flip], out_hbm.at[:, columns], sems.at[2 * number + flip]
            )
            copy.start()
            copies.append(copy)
    for copy in copies:
        copy.wait()


def place(offsets, pieces):
    return pl.pallas_call(
        functools.partial(place_kernel, offsets),
        out_specs=pl.BlockSpec(memory_space=pl.ANY),
        out_shape=jax.ShapeDtypeStruct((pieces[0].shape[1], HEADS * HDIM), jnp.bfloat16),
        scratch_shapes=[pltpu.SemaphoreType.DMA((2 * len(pieces),))],
    )(*[on_chip(piece) for piece in pieces])


def swapped(value, offset):
    count = lax.axis_size("seq")
    return lax.ppermute(value, "seq", [(source, source ^ offset) for source in range(count)])


def half_exchange(query_src, key_src, value_src, up_query, query_gain, key_gain, up_gain):
    far = HEADS // 2
    nears = tuple(range(0, far, 2))
    outgoing = pool_inputs(query_src, key_src, value_src, query_gain, key_gain)
    arrived = lax.all_to_all(outgoing, "seq", split_axis=0, concat_axis=0, tiled=True)
    queries = norm_up(up_query, up_gain, (0, PEER, far, far + PEER), nears)
    queries = dict(zip(nears, queries))
    for near in nears[1:]:
        queries[near] = swapped(queries[near], near)
    memory = short_attention(arrived, query_gain, key_gain)
    far_memory = swapped(memory, far)
    offsets, pieces = [], []
    for kind, held in enumerate((memory, far_memory)):
        peer_memory = swapped(held, PEER)
        done = attend(nears, [held], (2 * kind,), queries, None)
        done = attend(nears, [peer_memory], (2 * kind + 1,), queries, done)
        for near in nears:
            pieces.append(swapped(done[near], near) if near else done[near])
            offsets.append(near + kind * far)
    return place(tuple(offsets), pieces)


def local(*arrays):
    whole = lax.axis_size("seq") == HEADS and HEADS & (HEADS - 1) == 0
    return half_exchange(*arrays) if whole else head_exchange(*arrays)


def solution(mesh):
    in_specs = (
        P(("groups", "seq"), None),
        P(("groups", "seq"), None),
        P(("groups", "seq"), None),
        P(("groups", "seq"), None),
        P(),
        P(),
        P(),
    )
    out_specs = P(("groups", "seq"), None)
    return jax.shard_map(local, mesh=mesh, in_specs=in_specs, out_specs=out_specs, check_vma=False)
```

```python
import functools
import math

import jax
import jax.numpy as jnp
from jax import lax
from jax.experimental import pallas as pl
from jax.experimental.pallas import tpu as pltpu
from jax.sharding import PartitionSpec as P


HEADS = 16
HDIM = 128
SHORT = 4
SHIFT = 3


epsilon = 1e-06


def shifted(value, axis, steps):
    count = lax.axis_size(axis)
    leading, last = (max(0, -steps), min(count, count - steps))
    return lax.ppermute(value, axis, [(source, source + steps) for source in range(leading, last)])


def head_norm(values, gain_vector):
    row_count = values.shape[0]
    by_head = values.reshape(row_count, HEADS, HDIM)
    inverse_rms = lax.rsqrt(jnp.mean(by_head * by_head, axis=2, keepdims=True) + epsilon)
    return (by_head * inverse_rms * gain_vector.reshape(1, HEADS, HDIM)).reshape(
        row_count, HEADS * HDIM
    )


def row_norm(values):
    return values * lax.rsqrt(jnp.mean(values * values, axis=-1, keepdims=True) + epsilon)


def pooled_rows(source, edge_rows):
    widened = jnp.concatenate([edge_rows, source[: source.shape[0] - SHIFT]], axis=0).astype(
        jnp.float32
    )
    return jnp.mean(widened.reshape(-1, SHORT, widened.shape[1]), axis=1)


def blocked_attention(queries, query_limit, key_rows, value_rows, key_positions, block_size):
    head_count, query_count, head_size = queries.shape
    block_total = key_rows.shape[1] // block_size
    ceiling = jnp.max(query_limit)

    def visit_block(block_index, totals):
        offset = block_index * block_size
        block_pos = lax.dynamic_slice_in_dim(key_positions, offset, block_size, 0)

        def compute(state):
            numer_in, denom_in = state
            key_block = lax.dynamic_slice_in_dim(key_rows, offset, block_size, 1)
            value_block = lax.dynamic_slice_in_dim(value_rows, offset, block_size, 1)
            scores = jnp.einsum(
                "hqd,hkd->hqk", queries, key_block, preferred_element_type=jnp.float32
            ) / math.sqrt(HDIM)
            visible = block_pos[None, :] <= query_limit[:, None]
            exponent = jnp.where(visible[None], jnp.exp(scores), 0.0)
            denom_out = denom_in + jnp.sum(exponent, axis=2)
            numer_out = numer_in + jnp.einsum(
                "hqk,hkd->hqd",
                exponent.astype(jnp.bfloat16),
                value_block,
                preferred_element_type=jnp.float32,
            )
            return (numer_out, denom_out)

        return lax.cond(jnp.min(block_pos) <= ceiling, compute, lambda state: state, totals)

    initial = (
        jnp.zeros((head_count, query_count, head_size), jnp.float32),
        jnp.zeros((head_count, query_count), jnp.float32),
    )
    numerator, denominator = lax.fori_loop(0, block_total, visit_block, initial)
    return numerator / denominator[:, :, None]


def spread_heads(matrices, row_count, block_count, device_count):
    count = len(matrices)
    joined = jnp.stack(matrices).reshape(count, row_count, HEADS, HDIM)
    joined = jnp.transpose(joined, (2, 0, 1, 3)).reshape(HEADS, 1, count * row_count, HDIM)
    return jnp.broadcast_to(joined, (HEADS, block_count, count * row_count, HDIM)).reshape(
        device_count, count * row_count, HDIM
    )


def split_pieces(matrix, row_count, block_count, device_count):
    piece = row_count // block_count
    parted = matrix.reshape(block_count, piece, HEADS, HDIM)
    return jnp.transpose(parted, (2, 0, 1, 3)).reshape(device_count, piece, HDIM)


def head_exchange(query_src, key_src, value_src, up_query, query_gain, key_gain, up_gain):
    device_count = lax.axis_size("seq")
    device_index = lax.axis_index("seq")
    block_count = device_count // HEADS
    block_index = device_index % block_count
    token_count = query_src.shape[0]
    edges = jnp.stack(
        [
            query_src[token_count - SHIFT :],
            key_src[token_count - SHIFT :],
            value_src[token_count - SHIFT :],
        ]
    )
    edges = shifted(edges, "seq", 1)
    short_query = head_norm(pooled_rows(query_src, edges[0]), query_gain).astype(jnp.bfloat16)
    short_key = head_norm(pooled_rows(key_src, edges[1]), key_gain).astype(jnp.bfloat16)
    short_value = pooled_rows(value_src, edges[2]).astype(jnp.bfloat16)
    row_count = short_query.shape[0]
    up_heads = head_norm(up_query.astype(jnp.float32), up_gain).astype(jnp.bfloat16)
    row_total = row_count * device_count
    key_block = math.gcd(512, row_total)
    row_positions = jnp.arange(row_total, dtype=jnp.int32)
    device_rows = jnp.arange(device_count, dtype=jnp.int32)[:, None]
    qkv_out = spread_heads(
        [short_query, short_key, short_value], row_count, block_count, device_count
    )
    up_out = split_pieces(up_heads, token_count, block_count, device_count)
    arrived, own_up = (
        lax.all_to_all(qkv_out, "seq", split_axis=0, concat_axis=0, tiled=True),
        lax.all_to_all(up_out, "seq", split_axis=0, concat_axis=0, tiled=True),
    )
    all_query = arrived[:, :row_count].reshape(row_total, HDIM)
    all_key = arrived[:, row_count : 2 * row_count].reshape(row_total, HDIM)
    all_value = arrived[:, 2 * row_count :].reshape(row_total, HDIM)

    def fill_block(index_now, memory_now):
        offset = index_now * key_block
        block_query = lax.dynamic_slice_in_dim(all_query, offset, key_block, 0)[None]
        limits = offset + jnp.arange(key_block, dtype=jnp.int32)
        attended = blocked_attention(
            block_query, limits, all_key[None], all_value[None], row_positions, key_block
        )[0]
        return lax.dynamic_update_slice_in_dim(
            memory_now, row_norm(attended).astype(jnp.bfloat16), offset, 0
        )

    memory = lax.fori_loop(
        0, row_total // key_block, fill_block, jnp.zeros((row_total, HDIM), jnp.bfloat16)
    )
    token_piece = token_count // block_count
    own_tokens = (
        device_rows * token_count
        + block_index * token_piece
        + jnp.arange(token_piece, dtype=jnp.int32)[None, :]
    ).reshape(-1)
    own_up = own_up.reshape(1, device_count * token_piece, HDIM)
    result = blocked_attention(
        own_up, own_tokens // SHORT, memory[None], memory[None], row_positions, key_block
    )[0]
    result = result.astype(jnp.bfloat16).reshape(device_count, token_piece, HDIM)
    returned = lax.all_to_all(result, "seq", split_axis=0, concat_axis=0, tiled=True)
    output_heads = returned.reshape(HEADS, token_count, HDIM)
    return jnp.transpose(output_heads, (1, 0, 2)).reshape(token_count, HEADS * HDIM)


EDGE_ROWS = 3 * SHIFT - 1
PEER = 1


def rms_rows(values):
    return values * lax.rsqrt(jnp.mean(values * values, axis=-1, keepdims=True) + epsilon)


def on_chip(value):
    return pltpu.with_memory_space_constraint(value, pltpu.VMEM)


def select_matrix(tokens, rows, slot):
    row = lax.broadcasted_iota(jnp.int32, (rows + EDGE_ROWS, tokens), 0)
    col = lax.broadcasted_iota(jnp.int32, (rows + EDGE_ROWS, tokens), 1)
    pooled = (row < rows) & (col <= SHORT * row) & (col >= SHORT * row - SHIFT)
    weight = jnp.where(row == 0, 1.0, 1.0 / SHORT)
    edge = (row >= rows + slot * SHIFT) & (row < rows + (slot + 1) * SHIFT)
    last = col >= tokens - SHIFT
    if slot < 2:
        last = col == tokens - SHIFT + row - rows - slot * SHIFT
    return jnp.where(pooled, weight, jnp.where(edge & last, 1.0, 0.0)).astype(jnp.bfloat16)


def pool_kernel(*refs):
    sources, out_hbm = refs[:5], refs[5]
    buffers, out_ref, in_sems, out_sems = refs[6:11], refs[11], refs[12], refs[13]
    tokens, columns = sources[0].shape
    rows = tokens // SHORT
    copies = [
        pltpu.make_async_copy(source, buffer, in_sems.at[index])
        for index, (source, buffer) in enumerate(zip(sources, buffers))
    ]
    for index in (0, 3, 1, 4, 2):
        copies[index].start()
    picks = [select_matrix(tokens, rows, slot) for slot in range(3)]
    first = lax.broadcasted_iota(jnp.int32, (rows, HDIM), 0) == 0
    rest = lax.broadcasted_iota(jnp.int32, (EDGE_ROWS, HDIM), 0) == EDGE_ROWS - 1
    edges, returns = [], []
    for slot in range(3):
        copies[slot].wait()
        if slot < 2:
            copies[3 + slot].wait()
        picked = jnp.dot(picks[slot], buffers[slot][...], preferred_element_type=jnp.float32)
        edges.append(picked[rows:])
        span = rows if slot < 2 else rows + EDGE_ROWS
        for head in range(columns // HDIM):
            inside = slice(head * HDIM, (head + 1) * HDIM)
            part = picked[:rows, inside]
            if slot < 2:
                gain = buffers[3 + slot][head : head + 1, :]
                part = jnp.where(first, part, rms_rows(part) * gain)
            else:
                edge = sum(values[:, inside] for values in edges)
                high = edge.astype(jnp.bfloat16)
                low = (edge - high.astype(jnp.float32)).astype(jnp.bfloat16)
                out_ref[head, 3 * rows :, :] = jnp.where(rest, low, high)
            out_ref[head, slot * rows : (slot + 1) * rows, :] = part.astype(jnp.bfloat16)
        target = pl.ds(slot * rows, span)
        copy = pltpu.make_async_copy(
            out_ref.at[:, target], out_hbm.at[:, target], out_sems.at[slot]
        )
        copy.start()
        returns.append(copy)
    for copy in returns:
        copy.wait()


def pool_inputs(query_src, key_src, value_src, query_gain, key_gain):
    tokens, columns = query_src.shape
    heads = columns // HDIM
    depth = 3 * (tokens // SHORT) + EDGE_ROWS
    return pl.pallas_call(
        pool_kernel,
        in_specs=[pl.BlockSpec(memory_space=pl.ANY)] * 5,
        out_specs=pl.BlockSpec(memory_space=pl.ANY),
        out_shape=jax.ShapeDtypeStruct((heads, depth, HDIM), jnp.bfloat16),
        scratch_shapes=[pltpu.VMEM((tokens, columns), jnp.bfloat16)] * 3
        + [pltpu.VMEM((heads, HDIM), jnp.float32)] * 2
        + [pltpu.VMEM((heads, depth, HDIM), jnp.bfloat16)]
        + [pltpu.SemaphoreType.DMA((5,)), pltpu.SemaphoreType.DMA((3,))],
    )(query_src, key_src, value_src, query_gain.reshape(heads, HDIM), key_gain.reshape(heads, HDIM))


def scaled_exp(scores):
    return jnp.exp2(scores * (math.log2(math.e) / math.sqrt(HDIM)))


def across(left, right):
    return lax.dot_general(
        left, right, (((1,), (1,)), ((), ())), preferred_element_type=jnp.float32
    )


def short_kernel(block, arrived_ref, query_gain_ref, key_gain_ref, memory_ref):
    count, depth, _ = arrived_ref.shape
    rows = (depth - EDGE_ROWS) // 3
    total = count * rows
    head = lax.axis_index("seq")
    edges = arrived_ref[:, 3 * rows :, :].astype(jnp.float32)
    edge_row = lax.broadcasted_iota(jnp.int32, edges.shape, 1)
    first = lax.broadcasted_iota(jnp.int32, (count, rows, HDIM), 1) == 0
    tensors = []
    for slot, gain_ref in enumerate((query_gain_ref, key_gain_ref, None)):
        part = arrived_ref[:, slot * rows : (slot + 1) * rows, :].astype(jnp.float32)
        own = (edge_row >= slot * SHIFT) & (edge_row < (slot + 1) * SHIFT)
        tail = jnp.sum(jnp.where(own, edges, 0.0), axis=1, keepdims=True)
        before = jnp.concatenate([jnp.zeros_like(tail[:1]), tail[:-1]], axis=0)
        mean = (before + part[:, :1, :]) * (1.0 / SHORT)
        if gain_ref is not None:
            mean = rms_rows(mean) * gain_ref[pl.ds(head, 1), :][None]
        part = jnp.where(first, mean, part).astype(jnp.bfloat16)
        tensors.append(part.reshape(total, HDIM))
    query, key, value = tensors
    diagonal = lax.broadcasted_iota(jnp.int32, (block, block), 1) <= lax.broadcasted_iota(
        jnp.int32, (block, block), 0
    )
    starts = range(0, total, block)
    sums = [0.0] * len(starts)
    numerators = [0.0] * len(starts)
    for index, start in enumerate(starts):
        exponent = scaled_exp(across(query[start:], key[start : start + block]))
        for later in range(index, len(starts)):
            offset = (later - index) * block
            part = exponent[offset : offset + block]
            if later == index:
                part = jnp.where(diagonal, part, 0.0)
            sums[later] += part
            numerators[later] += jnp.dot(
                part.astype(jnp.bfloat16),
                value[start : start + block],
                preferred_element_type=jnp.float32,
            )
    for index, start in enumerate(starts):
        denominator = jnp.sum(sums[index], axis=1, keepdims=True)
        memory_ref[start : start + block, :] = rms_rows(numerators[index] / denominator).astype(
            jnp.bfloat16
        )


def short_attention(arrived, query_gain, key_gain):
    count, depth, _ = arrived.shape
    row_total = count * (depth - EDGE_ROWS) // 3
    return pl.pallas_call(
        functools.partial(short_kernel, math.gcd(128, row_total)),
        out_shape=pltpu.VMEM((row_total, HDIM), jnp.bfloat16),
    )(on_chip(arrived), *[on_chip(gain.reshape(-1, HDIM)) for gain in (query_gain, key_gain)])


def norm_kernel(shifts, nears, up_ref, gain_ref, *out_refs):
    device = lax.axis_index("seq")
    for near, out_ref in zip(nears, out_refs):
        for index, shift in enumerate(shifts):
            head = device ^ (near + shift)
            columns = pl.ds(pl.multiple_of(head * HDIM, HDIM), HDIM)
            query = rms_rows(up_ref[:, columns].astype(jnp.float32)) * gain_ref[pl.ds(head, 1), :]
            out_ref[index] = query.astype(jnp.bfloat16)


def norm_up(up_query, up_gain, shifts, nears):
    tokens = up_query.shape[0]
    shape = pltpu.VMEM((len(shifts), tokens, HDIM), jnp.bfloat16)
    return pl.pallas_call(
        functools.partial(norm_kernel, shifts, nears), out_shape=[shape] * len(nears)
    )(up_query, up_gain.reshape(-1, HDIM))


def attend_kernel(nears, first, held, *refs):
    count = len(nears)
    memory_refs, refs = refs[: len(held)], refs[len(held) :]
    query_refs, out_refs = refs[:count], refs[-count:]
    done_refs = refs[count:-count]
    tokens = query_refs[0].shape[1]
    row_total = memory_refs[0].shape[0]
    device = lax.axis_index("seq")
    token = lax.broadcasted_iota(jnp.int32, (tokens, row_total), 0)
    column = SHORT * lax.broadcasted_iota(jnp.int32, (tokens, row_total), 1)
    behind = column - token
    for index, (memory_ref, slot) in enumerate(zip(memory_refs, held)):
        memory = memory_ref[...]
        query = jnp.concatenate([query_ref[slot] for query_ref in query_refs], axis=0)
        exponent = scaled_exp(across(query, memory))
        exponent = jnp.concatenate(
            [
                jnp.where(
                    behind <= (device ^ near) * tokens,
                    exponent[order * tokens : (order + 1) * tokens],
                    0.0,
                )
                for order, near in enumerate(nears)
            ],
            axis=0,
        )
        denominator = jnp.sum(exponent, axis=1, keepdims=True)
        numerator = jnp.dot(
            exponent.astype(jnp.bfloat16), memory, preferred_element_type=jnp.float32
        )
        result = (numerator / denominator).astype(jnp.bfloat16)
        for order, out_ref in enumerate(out_refs):
            out_ref[first + index] = result[order * tokens : (order + 1) * tokens]
    for done_ref, out_ref in zip(done_refs, out_refs):
        out_ref[:first] = done_ref[...]


def attend(nears, memories, held, queries, done):
    tokens = queries[nears[0]].shape[1]
    first = done[nears[0]].shape[0] if done else 0
    operands = [*memories, *[queries[near] for near in nears]]
    operands += [done[near] for near in nears] if done else []
    shape = pltpu.VMEM((first + len(held), tokens, HDIM), jnp.bfloat16)
    results = pl.pallas_call(
        functools.partial(attend_kernel, nears, first, held), out_shape=[shape] * len(nears)
    )(*[on_chip(value) for value in operands])
    return dict(zip(nears, results))


def place_kernel(offsets, *refs):
    piece_refs, out_hbm, sems = refs[:-2], refs[-2], refs[-1]
    device = lax.axis_index("seq")
    copies = []
    for number, (offset, piece_ref) in enumerate(zip(offsets, piece_refs)):
        for flip in (0, PEER):
            head = device ^ (offset + flip)
            columns = pl.ds(pl.multiple_of(head * HDIM, HDIM), HDIM)
            copy = pltpu.make_async_copy(
                piece_ref.at[flip], out_hbm.at[:, columns], sems.at[2 * number + flip]
            )
            copy.start()
            copies.append(copy)
    for copy in copies:
        copy.wait()


def place(offsets, pieces):
    return pl.pallas_call(
        functools.partial(place_kernel, offsets),
        out_specs=pl.BlockSpec(memory_space=pl.ANY),
        out_shape=jax.ShapeDtypeStruct((pieces[0].shape[1], HEADS * HDIM), jnp.bfloat16),
        scratch_shapes=[pltpu.SemaphoreType.DMA((2 * len(pieces),))],
    )(*[on_chip(piece) for piece in pieces])


def swapped(value, offset):
    count = lax.axis_size("seq")
    return lax.ppermute(value, "seq", [(source, source ^ offset) for source in range(count)])


def half_exchange(query_src, key_src, value_src, up_query, query_gain, key_gain, up_gain):
    far = HEADS // 2
    nears = tuple(range(0, far, 2))
    outgoing = pool_inputs(query_src, key_src, value_src, query_gain, key_gain)
    arrived = lax.all_to_all(outgoing, "seq", split_axis=0, concat_axis=0, tiled=True)
    queries = norm_up(up_query, up_gain, (0, PEER, far, far + PEER), nears)
    queries = dict(zip(nears, queries))
    for near in nears[1:]:
        queries[near] = swapped(queries[near], near)
    memory = short_attention(arrived, query_gain, key_gain)
    far_memory = swapped(memory, far)
    offsets, pieces = [], []
    for kind, held in enumerate((memory, far_memory)):
        peer_memory = swapped(held, PEER)
        done = attend(nears, [held], (2 * kind,), queries, None)
        done = attend(nears, [peer_memory], (2 * kind + 1,), queries, done)
        for near in nears:
            pieces.append(swapped(done[near], near) if near else done[near])
            offsets.append(near + kind * far)
    return place(tuple(offsets), pieces)


def local(*arrays):
    whole = lax.axis_size("seq") == HEADS and HEADS & (HEADS - 1) == 0
    return half_exchange(*arrays) if whole else head_exchange(*arrays)


def solution(mesh):
    in_specs = (
        P(("groups", "seq"), None),
        P(("groups", "seq"), None),
        P(("groups", "seq"), None),
        P(("groups", "seq"), None),
        P(),
        P(),
        P(),
    )
    out_specs = P(("groups", "seq"), None)
    return jax.shard_map(local, mesh=mesh, in_specs=in_specs, out_specs=out_specs, check_vma=False)
```

```python
import functools
import math

import jax
import jax.numpy as jnp
from jax import lax
from jax.experimental import pallas as pl
from jax.experimental.pallas import tpu as pltpu
from jax.sharding import PartitionSpec as P


HEADS = 16
HDIM = 128
SHORT = 4
SHIFT = 3


epsilon = 1e-06


def shifted(value, axis, steps):
    count = lax.axis_size(axis)
    leading, last = (max(0, -steps), min(count, count - steps))
    return lax.ppermute(value, axis, [(source, source + steps) for source in range(leading, last)])


def head_norm(values, gain_vector):
    row_count = values.shape[0]
    by_head = values.reshape(row_count, HEADS, HDIM)
    inverse_rms = lax.rsqrt(jnp.mean(by_head * by_head, axis=2, keepdims=True) + epsilon)
    return (by_head * inverse_rms * gain_vector.reshape(1, HEADS, HDIM)).reshape(
        row_count, HEADS * HDIM
    )


def row_norm(values):
    return values * lax.rsqrt(jnp.mean(values * values, axis=-1, keepdims=True) + epsilon)


def pooled_rows(source, edge_rows):
    widened = jnp.concatenate([edge_rows, source[: source.shape[0] - SHIFT]], axis=0).astype(
        jnp.float32
    )
    return jnp.mean(widened.reshape(-1, SHORT, widened.shape[1]), axis=1)


def blocked_attention(queries, query_limit, key_rows, value_rows, key_positions, block_size):
    head_count, query_count, head_size = queries.shape
    block_total = key_rows.shape[1] // block_size
    ceiling = jnp.max(query_limit)

    def visit_block(block_index, totals):
        offset = block_index * block_size
        block_pos = lax.dynamic_slice_in_dim(key_positions, offset, block_size, 0)

        def compute(state):
            numer_in, denom_in = state
            key_block = lax.dynamic_slice_in_dim(key_rows, offset, block_size, 1)
            value_block = lax.dynamic_slice_in_dim(value_rows, offset, block_size, 1)
            scores = jnp.einsum(
                "hqd,hkd->hqk", queries, key_block, preferred_element_type=jnp.float32
            ) / math.sqrt(HDIM)
            visible = block_pos[None, :] <= query_limit[:, None]
            exponent = jnp.where(visible[None], jnp.exp(scores), 0.0)
            denom_out = denom_in + jnp.sum(exponent, axis=2)
            numer_out = numer_in + jnp.einsum(
                "hqk,hkd->hqd",
                exponent.astype(jnp.bfloat16),
                value_block,
                preferred_element_type=jnp.float32,
            )
            return (numer_out, denom_out)

        return lax.cond(jnp.min(block_pos) <= ceiling, compute, lambda state: state, totals)

    initial = (
        jnp.zeros((head_count, query_count, head_size), jnp.float32),
        jnp.zeros((head_count, query_count), jnp.float32),
    )
    numerator, denominator = lax.fori_loop(0, block_total, visit_block, initial)
    return numerator / denominator[:, :, None]


def spread_heads(matrices, row_count, block_count, device_count):
    count = len(matrices)
    joined = jnp.stack(matrices).reshape(count, row_count, HEADS, HDIM)
    joined = jnp.transpose(joined, (2, 0, 1, 3)).reshape(HEADS, 1, count * row_count, HDIM)
    return jnp.broadcast_to(joined, (HEADS, block_count, count * row_count, HDIM)).reshape(
        device_count, count * row_count, HDIM
    )


def split_pieces(matrix, row_count, block_count, device_count):
    piece = row_count // block_count
    parted = matrix.reshape(block_count, piece, HEADS, HDIM)
    return jnp.transpose(parted, (2, 0, 1, 3)).reshape(device_count, piece, HDIM)


def head_exchange(query_src, key_src, value_src, up_query, query_gain, key_gain, up_gain):
    device_count = lax.axis_size("seq")
    device_index = lax.axis_index("seq")
    block_count = device_count // HEADS
    block_index = device_index % block_count
    token_count = query_src.shape[0]
    edges = jnp.stack(
        [
            query_src[token_count - SHIFT :],
            key_src[token_count - SHIFT :],
            value_src[token_count - SHIFT :],
        ]
    )
    edges = shifted(edges, "seq", 1)
    short_query = head_norm(pooled_rows(query_src, edges[0]), query_gain).astype(jnp.bfloat16)
    short_key = head_norm(pooled_rows(key_src, edges[1]), key_gain).astype(jnp.bfloat16)
    short_value = pooled_rows(value_src, edges[2]).astype(jnp.bfloat16)
    row_count = short_query.shape[0]
    up_heads = head_norm(up_query.astype(jnp.float32), up_gain).astype(jnp.bfloat16)
    row_total = row_count * device_count
    key_block = math.gcd(512, row_total)
    row_positions = jnp.arange(row_total, dtype=jnp.int32)
    device_rows = jnp.arange(device_count, dtype=jnp.int32)[:, None]
    qkv_out = spread_heads(
        [short_query, short_key, short_value], row_count, block_count, device_count
    )
    up_out = split_pieces(up_heads, token_count, block_count, device_count)
    arrived, own_up = (
        lax.all_to_all(qkv_out, "seq", split_axis=0, concat_axis=0, tiled=True),
        lax.all_to_all(up_out, "seq", split_axis=0, concat_axis=0, tiled=True),
    )
    all_query = arrived[:, :row_count].reshape(row_total, HDIM)
    all_key = arrived[:, row_count : 2 * row_count].reshape(row_total, HDIM)
    all_value = arrived[:, 2 * row_count :].reshape(row_total, HDIM)

    def fill_block(index_now, memory_now):
        offset = index_now * key_block
        block_query = lax.dynamic_slice_in_dim(all_query, offset, key_block, 0)[None]
        limits = offset + jnp.arange(key_block, dtype=jnp.int32)
        attended = blocked_attention(
            block_query, limits, all_key[None], all_value[None], row_positions, key_block
        )[0]
        return lax.dynamic_update_slice_in_dim(
            memory_now, row_norm(attended).astype(jnp.bfloat16), offset, 0
        )

    memory = lax.fori_loop(
        0, row_total // key_block, fill_block, jnp.zeros((row_total, HDIM), jnp.bfloat16)
    )
    token_piece = token_count // block_count
    own_tokens = (
        device_rows * token_count
        + block_index * token_piece
        + jnp.arange(token_piece, dtype=jnp.int32)[None, :]
    ).reshape(-1)
    own_up = own_up.reshape(1, device_count * token_piece, HDIM)
    result = blocked_attention(
        own_up, own_tokens // SHORT, memory[None], memory[None], row_positions, key_block
    )[0]
    result = result.astype(jnp.bfloat16).reshape(device_count, token_piece, HDIM)
    returned = lax.all_to_all(result, "seq", split_axis=0, concat_axis=0, tiled=True)
    output_heads = returned.reshape(HEADS, token_count, HDIM)
    return jnp.transpose(output_heads, (1, 0, 2)).reshape(token_count, HEADS * HDIM)


EDGE_ROWS = 3 * SHIFT - 1
PEER = 1


def rms_rows(values):
    return values * lax.rsqrt(jnp.mean(values * values, axis=-1, keepdims=True) + epsilon)


def on_chip(value):
    return pltpu.with_memory_space_constraint(value, pltpu.VMEM)


def select_matrix(tokens, rows, slot):
    row = lax.broadcasted_iota(jnp.int32, (rows + EDGE_ROWS, tokens), 0)
    col = lax.broadcasted_iota(jnp.int32, (rows + EDGE_ROWS, tokens), 1)
    pooled = (row < rows) & (col <= SHORT * row) & (col >= SHORT * row - SHIFT)
    weight = jnp.where(row == 0, 1.0, 1.0 / SHORT)
    edge = (row >= rows + slot * SHIFT) & (row < rows + (slot + 1) * SHIFT)
    last = col >= tokens - SHIFT
    if slot < 2:
        last = col == tokens - SHIFT + row - rows - slot * SHIFT
    return jnp.where(pooled, weight, jnp.where(edge & last, 1.0, 0.0)).astype(jnp.bfloat16)


def pool_kernel(*refs):
    sources, out_hbm = refs[:5], refs[5]
    buffers, out_ref, in_sems, out_sems = refs[6:11], refs[11], refs[12], refs[13]
    tokens, columns = sources[0].shape
    rows = tokens // SHORT
    copies = [
        pltpu.make_async_copy(source, buffer, in_sems.at[index])
        for index, (source, buffer) in enumerate(zip(sources, buffers))
    ]
    for index in (0, 3, 1, 4, 2):
        copies[index].start()
    picks = [select_matrix(tokens, rows, slot) for slot in range(3)]
    first = lax.broadcasted_iota(jnp.int32, (rows, HDIM), 0) == 0
    rest = lax.broadcasted_iota(jnp.int32, (EDGE_ROWS, HDIM), 0) == EDGE_ROWS - 1
    edges, returns = [], []
    for slot in range(3):
        copies[slot].wait()
        if slot < 2:
            copies[3 + slot].wait()
        picked = jnp.dot(picks[slot], buffers[slot][...], preferred_element_type=jnp.float32)
        edges.append(picked[rows:])
        span = rows if slot < 2 else rows + EDGE_ROWS
        for head in range(columns // HDIM):
            inside = slice(head * HDIM, (head + 1) * HDIM)
            part = picked[:rows, inside]
            if slot < 2:
                gain = buffers[3 + slot][head : head + 1, :]
                part = jnp.where(first, part, rms_rows(part) * gain)
            else:
                edge = sum(values[:, inside] for values in edges)
                high = edge.astype(jnp.bfloat16)
                low = (edge - high.astype(jnp.float32)).astype(jnp.bfloat16)
                out_ref[head, 3 * rows :, :] = jnp.where(rest, low, high)
            out_ref[head, slot * rows : (slot + 1) * rows, :] = part.astype(jnp.bfloat16)
        target = pl.ds(slot * rows, span)
        copy = pltpu.make_async_copy(
            out_ref.at[:, target], out_hbm.at[:, target], out_sems.at[slot]
        )
        copy.start()
        returns.append(copy)
    for copy in returns:
        copy.wait()


def pool_inputs(query_src, key_src, value_src, query_gain, key_gain):
    tokens, columns = query_src.shape
    heads = columns // HDIM
    depth = 3 * (tokens // SHORT) + EDGE_ROWS
    return pl.pallas_call(
        pool_kernel,
        in_specs=[pl.BlockSpec(memory_space=pl.ANY)] * 5,
        out_specs=pl.BlockSpec(memory_space=pl.ANY),
        out_shape=jax.ShapeDtypeStruct((heads, depth, HDIM), jnp.bfloat16),
        scratch_shapes=[pltpu.VMEM((tokens, columns), jnp.bfloat16)] * 3
        + [pltpu.VMEM((heads, HDIM), jnp.float32)] * 2
        + [pltpu.VMEM((heads, depth, HDIM), jnp.bfloat16)]
        + [pltpu.SemaphoreType.DMA((5,)), pltpu.SemaphoreType.DMA((3,))],
    )(query_src, key_src, value_src, query_gain.reshape(heads, HDIM), key_gain.reshape(heads, HDIM))


def scaled_exp(scores):
    return jnp.exp2(scores * (math.log2(math.e) / math.sqrt(HDIM)))


def across(left, right):
    return lax.dot_general(
        left, right, (((1,), (1,)), ((), ())), preferred_element_type=jnp.float32
    )


def short_kernel(block, arrived_ref, query_gain_ref, key_gain_ref, memory_ref, *half_refs):
    count, depth, _ = arrived_ref.shape
    rows = (depth - EDGE_ROWS) // 3
    total = count * rows
    head = lax.axis_index("seq")
    edges = arrived_ref[:, 3 * rows :, :].astype(jnp.float32)
    edge_row = lax.broadcasted_iota(jnp.int32, edges.shape, 1)
    first = lax.broadcasted_iota(jnp.int32, (count, rows, HDIM), 1) == 0
    tensors = []
    for slot, gain_ref in enumerate((query_gain_ref, key_gain_ref, None)):
        part = arrived_ref[:, slot * rows : (slot + 1) * rows, :].astype(jnp.float32)
        own = (edge_row >= slot * SHIFT) & (edge_row < (slot + 1) * SHIFT)
        tail = jnp.sum(jnp.where(own, edges, 0.0), axis=1, keepdims=True)
        before = jnp.concatenate([jnp.zeros_like(tail[:1]), tail[:-1]], axis=0)
        mean = (before + part[:, :1, :]) * (1.0 / SHORT)
        if gain_ref is not None:
            mean = rms_rows(mean) * gain_ref[pl.ds(head, 1), :][None]
        part = jnp.where(first, mean, part).astype(jnp.bfloat16)
        tensors.append(part.reshape(total, HDIM))
    query, key, value = tensors
    diagonal = lax.broadcasted_iota(jnp.int32, (block, block), 1) <= lax.broadcasted_iota(
        jnp.int32, (block, block), 0
    )
    starts = range(0, total, block)
    sums = [0.0] * len(starts)
    numerators = [0.0] * len(starts)
    for index, start in enumerate(starts):
        exponent = scaled_exp(across(query[start:], key[start : start + block]))
        for later in range(index, len(starts)):
            offset = (later - index) * block
            part = exponent[offset : offset + block]
            if later == index:
                part = jnp.where(diagonal, part, 0.0)
            sums[later] += part
            numerators[later] += jnp.dot(
                part.astype(jnp.bfloat16),
                value[start : start + block],
                preferred_element_type=jnp.float32,
            )
    for index, start in enumerate(starts):
        denominator = jnp.sum(sums[index], axis=1, keepdims=True)
        result = rms_rows(numerators[index] / denominator).astype(jnp.bfloat16)
        memory_ref[start : start + block, :] = result
        upper, inside = divmod(start, total // 2)
        half_refs[upper][inside : inside + block, :] = result


def short_attention(arrived, query_gain, key_gain):
    count, depth, _ = arrived.shape
    row_total = count * (depth - EDGE_ROWS) // 3
    return pl.pallas_call(
        functools.partial(short_kernel, math.gcd(128, row_total // 2)),
        out_shape=[
            pltpu.VMEM((size, HDIM), jnp.bfloat16)
            for size in (row_total, row_total // 2, row_total // 2)
        ],
    )(on_chip(arrived), *[on_chip(gain.reshape(-1, HDIM)) for gain in (query_gain, key_gain)])


def norm_kernel(shifts, nears, up_ref, gain_ref, *out_refs):
    device = lax.axis_index("seq")
    for near, out_ref in zip(nears, out_refs):
        for index, shift in enumerate(shifts):
            head = device ^ (near + shift)
            columns = pl.ds(pl.multiple_of(head * HDIM, HDIM), HDIM)
            query = rms_rows(up_ref[:, columns].astype(jnp.float32)) * gain_ref[pl.ds(head, 1), :]
            out_ref[index] = query.astype(jnp.bfloat16)


def norm_up(up_query, up_gain, shifts, nears):
    tokens = up_query.shape[0]
    shape = pltpu.VMEM((len(shifts), tokens, HDIM), jnp.bfloat16)
    return pl.pallas_call(
        functools.partial(norm_kernel, shifts, nears), out_shape=[shape] * len(nears)
    )(up_query, up_gain.reshape(-1, HDIM))


def attend_kernel(nears, slot, parts, *refs):
    count = len(nears)
    memory_refs, query_refs, refs = refs[:parts], refs[parts : parts + count], refs[parts + count :]
    done_refs, out_refs = refs[:-count], refs[-count:]
    tokens = query_refs[0].shape[1]
    memory = jnp.concatenate([memory_ref[...] for memory_ref in memory_refs], axis=0)
    row_total = memory.shape[0]
    device = lax.axis_index("seq")
    token = lax.broadcasted_iota(jnp.int32, (tokens, row_total), 0)
    column = SHORT * lax.broadcasted_iota(jnp.int32, (tokens, row_total), 1)
    behind = column - token
    query = jnp.concatenate([query_ref[slot] for query_ref in query_refs], axis=0)
    exponent = scaled_exp(across(query, memory))
    exponent = jnp.concatenate(
        [
            jnp.where(
                behind <= (device ^ near) * tokens,
                exponent[order * tokens : (order + 1) * tokens],
                0.0,
            )
            for order, near in enumerate(nears)
        ],
        axis=0,
    )
    denominator = jnp.sum(exponent, axis=1, keepdims=True)
    numerator = jnp.dot(exponent.astype(jnp.bfloat16), memory, preferred_element_type=jnp.float32)
    result = (numerator / denominator).astype(jnp.bfloat16)
    for order, out_ref in enumerate(out_refs):
        out_ref[out_ref.shape[0] - 1] = result[order * tokens : (order + 1) * tokens]
    for done_ref, out_ref in zip(done_refs, out_refs):
        out_ref[: done_ref.shape[0]] = done_ref[...]


def attend(nears, memory, slot, queries, done):
    tokens = queries[nears[0]].shape[1]
    operands = [*memory, *[queries[near] for near in nears]]
    operands += [done[near] for near in nears] if done else []
    shape = pltpu.VMEM((2 if done else 1, tokens, HDIM), jnp.bfloat16)
    results = pl.pallas_call(
        functools.partial(attend_kernel, nears, slot, len(memory)), out_shape=[shape] * len(nears)
    )(*[on_chip(value) for value in operands])
    return dict(zip(nears, results))


def place_kernel(offsets, *refs):
    piece_refs, out_hbm, sems = refs[:-2], refs[-2], refs[-1]
    device = lax.axis_index("seq")
    copies = []
    for number, (offset, piece_ref) in enumerate(zip(offsets, piece_refs)):
        for flip in (0, PEER):
            head = device ^ (offset + flip)
            columns = pl.ds(pl.multiple_of(head * HDIM, HDIM), HDIM)
            copy = pltpu.make_async_copy(
                piece_ref.at[flip], out_hbm.at[:, columns], sems.at[2 * number + flip]
            )
            copy.start()
            copies.append(copy)
    for copy in copies:
        copy.wait()


def place(offsets, pieces):
    return pl.pallas_call(
        functools.partial(place_kernel, offsets),
        out_specs=pl.BlockSpec(memory_space=pl.ANY),
        out_shape=jax.ShapeDtypeStruct((pieces[0].shape[1], HEADS * HDIM), jnp.bfloat16),
        scratch_shapes=[pltpu.SemaphoreType.DMA((2 * len(pieces),))],
    )(*[on_chip(piece) for piece in pieces])


def swapped(value, offset):
    count = lax.axis_size("seq")
    return lax.ppermute(value, "seq", [(source, source ^ offset) for source in range(count)])


def half_exchange(query_src, key_src, value_src, up_query, query_gain, key_gain, up_gain):
    far = HEADS // 2
    nears = tuple(range(0, far, 2))
    outgoing = pool_inputs(query_src, key_src, value_src, query_gain, key_gain)
    arrived = lax.all_to_all(outgoing, "seq", split_axis=0, concat_axis=0, tiled=True)
    queries = norm_up(up_query, up_gain, (0, PEER, far, far + PEER), nears)
    queries = dict(zip(nears, queries))
    for near in nears[1:]:
        queries[near] = swapped(queries[near], near)
    memory, lower, upper = short_attention(arrived, query_gain, key_gain)
    far_lower = swapped(lower, far)
    far_upper = lax.ppermute(upper, "seq", [(source, source + far) for source in range(far)])
    offsets, pieces = [], []
    for kind, held in enumerate(([memory], [far_lower, far_upper])):
        peer_memory = []
        for value in held:
            peer_memory.append(swapped(value, PEER))
        done = attend(nears, held, 2 * kind, queries, None)
        done = attend(nears, peer_memory, 2 * kind + 1, queries, done)
        for near in nears:
            pieces.append(swapped(done[near], near) if near else done[near])
            offsets.append(near + kind * far)
    return place(tuple(offsets), pieces)


def local(*arrays):
    whole = lax.axis_size("seq") == HEADS and HEADS & (HEADS - 1) == 0
    return half_exchange(*arrays) if whole else head_exchange(*arrays)


def solution(mesh):
    in_specs = (
        P(("groups", "seq"), None),
        P(("groups", "seq"), None),
        P(("groups", "seq"), None),
        P(("groups", "seq"), None),
        P(),
        P(),
        P(),
    )
    out_specs = P(("groups", "seq"), None)
    return jax.shard_map(local, mesh=mesh, in_specs=in_specs, out_specs=out_specs, check_vma=False)
```

```python
import functools
import math

import jax
import jax.numpy as jnp
from jax import lax
from jax.experimental import pallas as pl
from jax.experimental.pallas import tpu as pltpu
from jax.sharding import PartitionSpec as P


HEADS = 16
HDIM = 128
SHORT = 4
SHIFT = 3


epsilon = 1e-06


def shifted(value, axis, steps):
    count = lax.axis_size(axis)
    leading, last = (max(0, -steps), min(count, count - steps))
    return lax.ppermute(value, axis, [(source, source + steps) for source in range(leading, last)])


def head_norm(values, gain_vector):
    row_count = values.shape[0]
    by_head = values.reshape(row_count, HEADS, HDIM)
    inverse_rms = lax.rsqrt(jnp.mean(by_head * by_head, axis=2, keepdims=True) + epsilon)
    return (by_head * inverse_rms * gain_vector.reshape(1, HEADS, HDIM)).reshape(
        row_count, HEADS * HDIM
    )


def row_norm(values):
    return values * lax.rsqrt(jnp.mean(values * values, axis=-1, keepdims=True) + epsilon)


def pooled_rows(source, edge_rows):
    widened = jnp.concatenate([edge_rows, source[: source.shape[0] - SHIFT]], axis=0).astype(
        jnp.float32
    )
    return jnp.mean(widened.reshape(-1, SHORT, widened.shape[1]), axis=1)


def blocked_attention(queries, query_limit, key_rows, value_rows, key_positions, block_size):
    head_count, query_count, head_size = queries.shape
    block_total = key_rows.shape[1] // block_size
    ceiling = jnp.max(query_limit)

    def visit_block(block_index, totals):
        offset = block_index * block_size
        block_pos = lax.dynamic_slice_in_dim(key_positions, offset, block_size, 0)

        def compute(state):
            numer_in, denom_in = state
            key_block = lax.dynamic_slice_in_dim(key_rows, offset, block_size, 1)
            value_block = lax.dynamic_slice_in_dim(value_rows, offset, block_size, 1)
            scores = jnp.einsum(
                "hqd,hkd->hqk", queries, key_block, preferred_element_type=jnp.float32
            ) / math.sqrt(HDIM)
            visible = block_pos[None, :] <= query_limit[:, None]
            exponent = jnp.where(visible[None], jnp.exp(scores), 0.0)
            denom_out = denom_in + jnp.sum(exponent, axis=2)
            numer_out = numer_in + jnp.einsum(
                "hqk,hkd->hqd",
                exponent.astype(jnp.bfloat16),
                value_block,
                preferred_element_type=jnp.float32,
            )
            return (numer_out, denom_out)

        return lax.cond(jnp.min(block_pos) <= ceiling, compute, lambda state: state, totals)

    initial = (
        jnp.zeros((head_count, query_count, head_size), jnp.float32),
        jnp.zeros((head_count, query_count), jnp.float32),
    )
    numerator, denominator = lax.fori_loop(0, block_total, visit_block, initial)
    return numerator / denominator[:, :, None]


def spread_heads(matrices, row_count, block_count, device_count):
    count = len(matrices)
    joined = jnp.stack(matrices).reshape(count, row_count, HEADS, HDIM)
    joined = jnp.transpose(joined, (2, 0, 1, 3)).reshape(HEADS, 1, count * row_count, HDIM)
    return jnp.broadcast_to(joined, (HEADS, block_count, count * row_count, HDIM)).reshape(
        device_count, count * row_count, HDIM
    )


def split_pieces(matrix, row_count, block_count, device_count):
    piece = row_count // block_count
    parted = matrix.reshape(block_count, piece, HEADS, HDIM)
    return jnp.transpose(parted, (2, 0, 1, 3)).reshape(device_count, piece, HDIM)


def head_exchange(query_src, key_src, value_src, up_query, query_gain, key_gain, up_gain):
    device_count = lax.axis_size("seq")
    device_index = lax.axis_index("seq")
    block_count = device_count // HEADS
    block_index = device_index % block_count
    token_count = query_src.shape[0]
    edges = jnp.stack(
        [
            query_src[token_count - SHIFT :],
            key_src[token_count - SHIFT :],
            value_src[token_count - SHIFT :],
        ]
    )
    edges = shifted(edges, "seq", 1)
    short_query = head_norm(pooled_rows(query_src, edges[0]), query_gain).astype(jnp.bfloat16)
    short_key = head_norm(pooled_rows(key_src, edges[1]), key_gain).astype(jnp.bfloat16)
    short_value = pooled_rows(value_src, edges[2]).astype(jnp.bfloat16)
    row_count = short_query.shape[0]
    up_heads = head_norm(up_query.astype(jnp.float32), up_gain).astype(jnp.bfloat16)
    row_total = row_count * device_count
    key_block = math.gcd(512, row_total)
    row_positions = jnp.arange(row_total, dtype=jnp.int32)
    device_rows = jnp.arange(device_count, dtype=jnp.int32)[:, None]
    qkv_out = spread_heads(
        [short_query, short_key, short_value], row_count, block_count, device_count
    )
    up_out = split_pieces(up_heads, token_count, block_count, device_count)
    arrived, own_up = (
        lax.all_to_all(qkv_out, "seq", split_axis=0, concat_axis=0, tiled=True),
        lax.all_to_all(up_out, "seq", split_axis=0, concat_axis=0, tiled=True),
    )
    all_query = arrived[:, :row_count].reshape(row_total, HDIM)
    all_key = arrived[:, row_count : 2 * row_count].reshape(row_total, HDIM)
    all_value = arrived[:, 2 * row_count :].reshape(row_total, HDIM)

    def fill_block(index_now, memory_now):
        offset = index_now * key_block
        block_query = lax.dynamic_slice_in_dim(all_query, offset, key_block, 0)[None]
        limits = offset + jnp.arange(key_block, dtype=jnp.int32)
        attended = blocked_attention(
            block_query, limits, all_key[None], all_value[None], row_positions, key_block
        )[0]
        return lax.dynamic_update_slice_in_dim(
            memory_now, row_norm(attended).astype(jnp.bfloat16), offset, 0
        )

    memory = lax.fori_loop(
        0, row_total // key_block, fill_block, jnp.zeros((row_total, HDIM), jnp.bfloat16)
    )
    token_piece = token_count // block_count
    own_tokens = (
        device_rows * token_count
        + block_index * token_piece
        + jnp.arange(token_piece, dtype=jnp.int32)[None, :]
    ).reshape(-1)
    own_up = own_up.reshape(1, device_count * token_piece, HDIM)
    result = blocked_attention(
        own_up, own_tokens // SHORT, memory[None], memory[None], row_positions, key_block
    )[0]
    result = result.astype(jnp.bfloat16).reshape(device_count, token_piece, HDIM)
    returned = lax.all_to_all(result, "seq", split_axis=0, concat_axis=0, tiled=True)
    output_heads = returned.reshape(HEADS, token_count, HDIM)
    return jnp.transpose(output_heads, (1, 0, 2)).reshape(token_count, HEADS * HDIM)


EDGE_ROWS = 3 * SHIFT - 1
PEER = 1


def rms_rows(values):
    return values * lax.rsqrt(jnp.mean(values * values, axis=-1, keepdims=True) + epsilon)


def on_chip(value):
    return pltpu.with_memory_space_constraint(value, pltpu.VMEM)


def select_matrix(tokens, rows, slot):
    row = lax.broadcasted_iota(jnp.int32, (rows + EDGE_ROWS, tokens), 0)
    col = lax.broadcasted_iota(jnp.int32, (rows + EDGE_ROWS, tokens), 1)
    pooled = (row < rows) & (col <= SHORT * row) & (col >= SHORT * row - SHIFT)
    weight = jnp.where(row == 0, 1.0, 1.0 / SHORT)
    edge = (row >= rows + slot * SHIFT) & (row < rows + (slot + 1) * SHIFT)
    last = col >= tokens - SHIFT
    if slot < 2:
        last = col == tokens - SHIFT + row - rows - slot * SHIFT
    return jnp.where(pooled, weight, jnp.where(edge & last, 1.0, 0.0)).astype(jnp.bfloat16)


def pool_kernel(*refs):
    sources, out_hbm = refs[:5], refs[5]
    buffers, out_ref, in_sems, out_sems = refs[6:11], refs[11], refs[12], refs[13]
    tokens, columns = sources[0].shape
    rows = tokens // SHORT
    copies = [
        pltpu.make_async_copy(source, buffer, in_sems.at[index])
        for index, (source, buffer) in enumerate(zip(sources, buffers))
    ]
    for index in (0, 3, 1, 4, 2):
        copies[index].start()
    picks = [select_matrix(tokens, rows, slot) for slot in range(3)]
    first = lax.broadcasted_iota(jnp.int32, (rows, HDIM), 0) == 0
    rest = lax.broadcasted_iota(jnp.int32, (EDGE_ROWS, HDIM), 0) == EDGE_ROWS - 1
    edges, returns = [], []
    for slot in range(3):
        copies[slot].wait()
        if slot < 2:
            copies[3 + slot].wait()
        picked = jnp.dot(picks[slot], buffers[slot][...], preferred_element_type=jnp.float32)
        edges.append(picked[rows:])
        span = rows if slot < 2 else rows + EDGE_ROWS
        for head in range(columns // HDIM):
            inside = slice(head * HDIM, (head + 1) * HDIM)
            part = picked[:rows, inside]
            if slot < 2:
                gain = buffers[3 + slot][head : head + 1, :]
                part = jnp.where(first, part, rms_rows(part) * gain)
            else:
                edge = sum(values[:, inside] for values in edges)
                high = edge.astype(jnp.bfloat16)
                low = (edge - high.astype(jnp.float32)).astype(jnp.bfloat16)
                out_ref[head, 3 * rows :, :] = jnp.where(rest, low, high)
            out_ref[head, slot * rows : (slot + 1) * rows, :] = part.astype(jnp.bfloat16)
        target = pl.ds(slot * rows, span)
        copy = pltpu.make_async_copy(
            out_ref.at[:, target], out_hbm.at[:, target], out_sems.at[slot]
        )
        copy.start()
        returns.append(copy)
    for copy in returns:
        copy.wait()


def pool_inputs(query_src, key_src, value_src, query_gain, key_gain):
    tokens, columns = query_src.shape
    heads = columns // HDIM
    depth = 3 * (tokens // SHORT) + EDGE_ROWS
    return pl.pallas_call(
        pool_kernel,
        in_specs=[pl.BlockSpec(memory_space=pl.ANY)] * 5,
        out_specs=pl.BlockSpec(memory_space=pl.ANY),
        out_shape=jax.ShapeDtypeStruct((heads, depth, HDIM), jnp.bfloat16),
        scratch_shapes=[pltpu.VMEM((tokens, columns), jnp.bfloat16)] * 3
        + [pltpu.VMEM((heads, HDIM), jnp.float32)] * 2
        + [pltpu.VMEM((heads, depth, HDIM), jnp.bfloat16)]
        + [pltpu.SemaphoreType.DMA((5,)), pltpu.SemaphoreType.DMA((3,))],
    )(query_src, key_src, value_src, query_gain.reshape(heads, HDIM), key_gain.reshape(heads, HDIM))


def scaled_exp(scores):
    return jnp.exp2(scores * (math.log2(math.e) / math.sqrt(HDIM)))


def across(left, right):
    return lax.dot_general(
        left, right, (((1,), (1,)), ((), ())), preferred_element_type=jnp.float32
    )


def short_kernel(block, arrived_ref, query_gain_ref, key_gain_ref, memory_ref):
    count, depth, _ = arrived_ref.shape
    rows = (depth - EDGE_ROWS) // 3
    total = count * rows
    head = lax.axis_index("seq")
    edges = arrived_ref[:, 3 * rows :, :].astype(jnp.float32)
    edge_row = lax.broadcasted_iota(jnp.int32, edges.shape, 1)
    first = lax.broadcasted_iota(jnp.int32, (count, rows, HDIM), 1) == 0
    tensors = []
    for slot, gain_ref in enumerate((query_gain_ref, key_gain_ref, None)):
        part = arrived_ref[:, slot * rows : (slot + 1) * rows, :].astype(jnp.float32)
        own = (edge_row >= slot * SHIFT) & (edge_row < (slot + 1) * SHIFT)
        tail = jnp.sum(jnp.where(own, edges, 0.0), axis=1, keepdims=True)
        before = jnp.concatenate([jnp.zeros_like(tail[:1]), tail[:-1]], axis=0)
        mean = (before + part[:, :1, :]) * (1.0 / SHORT)
        if gain_ref is not None:
            mean = rms_rows(mean) * gain_ref[pl.ds(head, 1), :][None]
        part = jnp.where(first, mean, part).astype(jnp.bfloat16)
        tensors.append(part.reshape(total, HDIM))
    query, key, value = tensors
    diagonal = lax.broadcasted_iota(jnp.int32, (block, block), 1) <= lax.broadcasted_iota(
        jnp.int32, (block, block), 0
    )
    starts = range(0, total, block)
    sums = [0.0] * len(starts)
    numerators = [0.0] * len(starts)
    for index, start in enumerate(starts):
        exponent = scaled_exp(across(query[start:], key[start : start + block]))
        for later in range(index, len(starts)):
            offset = (later - index) * block
            part = exponent[offset : offset + block]
            if later == index:
                part = jnp.where(diagonal, part, 0.0)
            sums[later] += part
            numerators[later] += jnp.dot(
                part.astype(jnp.bfloat16),
                value[start : start + block],
                preferred_element_type=jnp.float32,
            )
    for index, start in enumerate(starts):
        denominator = jnp.sum(sums[index], axis=1, keepdims=True)
        memory_ref[start : start + block, :] = rms_rows(numerators[index] / denominator).astype(
            jnp.bfloat16
        )


def short_attention(arrived, query_gain, key_gain):
    count, depth, _ = arrived.shape
    row_total = count * (depth - EDGE_ROWS) // 3
    return pl.pallas_call(
        functools.partial(short_kernel, math.gcd(128, row_total)),
        out_shape=pltpu.VMEM((row_total, HDIM), jnp.bfloat16),
    )(on_chip(arrived), *[on_chip(gain.reshape(-1, HDIM)) for gain in (query_gain, key_gain)])


def norm_kernel(shifts, nears, up_ref, gain_ref, *out_refs):
    device = lax.axis_index("seq")
    for near, out_ref in zip(nears, out_refs):
        for index, shift in enumerate(shifts):
            head = device ^ near ^ shift
            columns = pl.ds(pl.multiple_of(head * HDIM, HDIM), HDIM)
            query = rms_rows(up_ref[:, columns].astype(jnp.float32)) * gain_ref[pl.ds(head, 1), :]
            out_ref[index] = query.astype(jnp.bfloat16)


def norm_up(up_query, up_gain, shifts, nears):
    tokens = up_query.shape[0]
    shape = pltpu.VMEM((len(shifts), tokens, HDIM), jnp.bfloat16)
    return pl.pallas_call(
        functools.partial(norm_kernel, shifts, nears), out_shape=[shape] * len(nears)
    )(up_query, up_gain.reshape(-1, HDIM))


def attend_kernel(nears, slot, *refs):
    count = len(nears)
    memory_ref, query_refs, refs = refs[0], refs[1 : count + 1], refs[count + 1 :]
    done_refs, out_refs = refs[:-count], refs[-count:]
    tokens = query_refs[0].shape[1]
    row_total = memory_ref.shape[0]
    device = lax.axis_index("seq")

    def attend_rows(rows):
        memory = memory_ref[:rows]
        token = lax.broadcasted_iota(jnp.int32, (tokens, rows), 0)
        behind = SHORT * lax.broadcasted_iota(jnp.int32, (tokens, rows), 1) - token
        query = jnp.concatenate([query_ref[slot] for query_ref in query_refs], axis=0)
        exponent = scaled_exp(across(query, memory))
        exponent = jnp.concatenate(
            [
                jnp.where(
                    behind <= (device ^ near) * tokens,
                    exponent[order * tokens : (order + 1) * tokens],
                    0.0,
                )
                for order, near in enumerate(nears)
            ],
            axis=0,
        )
        denominator = jnp.sum(exponent, axis=1, keepdims=True)
        numerator = jnp.dot(
            exponent.astype(jnp.bfloat16), memory, preferred_element_type=jnp.float32
        )
        result = (numerator / denominator).astype(jnp.bfloat16)
        for order, out_ref in enumerate(out_refs):
            out_ref[out_ref.shape[0] - 1] = result[order * tokens : (order + 1) * tokens]

    @pl.when(device < HEADS // 2)
    def _():
        attend_rows(row_total // 2)

    @pl.when(device >= HEADS // 2)
    def _():
        attend_rows(row_total)

    for done_ref, out_ref in zip(done_refs, out_refs):
        out_ref[: done_ref.shape[0]] = done_ref[...]


def attend(nears, memory, slot, queries, done):
    tokens = queries[nears[0]].shape[1]
    operands = [memory, *[queries[near] for near in nears]]
    operands += [done[near] for near in nears] if done else []
    shape = pltpu.VMEM((2 if done else 1, tokens, HDIM), jnp.bfloat16)
    results = pl.pallas_call(
        functools.partial(attend_kernel, nears, slot), out_shape=[shape] * len(nears)
    )(*[on_chip(value) for value in operands])
    return dict(zip(nears, results))


def place_kernel(offsets, *refs):
    piece_refs, out_hbm, sems = refs[:-2], refs[-2], refs[-1]
    device = lax.axis_index("seq")
    copies = []
    for number, (offset, piece_ref) in enumerate(zip(offsets, piece_refs)):
        for flip in (0, PEER):
            head = device ^ offset ^ flip
            columns = pl.ds(pl.multiple_of(head * HDIM, HDIM), HDIM)
            copy = pltpu.make_async_copy(
                piece_ref.at[flip], out_hbm.at[:, columns], sems.at[2 * number + flip]
            )
            copy.start()
            copies.append(copy)
    for copy in copies:
        copy.wait()


def place(offsets, pieces):
    return pl.pallas_call(
        functools.partial(place_kernel, offsets),
        out_specs=pl.BlockSpec(memory_space=pl.ANY),
        out_shape=jax.ShapeDtypeStruct((pieces[0].shape[1], HEADS * HDIM), jnp.bfloat16),
        scratch_shapes=[pltpu.SemaphoreType.DMA((2 * len(pieces),))],
    )(*[on_chip(piece) for piece in pieces])


def swapped(value, offset):
    count = lax.axis_size("seq")
    return lax.ppermute(value, "seq", [(source, source ^ offset) for source in range(count)])


def half_exchange(query_src, key_src, value_src, up_query, query_gain, key_gain, up_gain):
    far = HEADS // 2 + HEADS // 4
    nears = tuple(range(0, HEADS // 2, 2))
    outgoing = pool_inputs(query_src, key_src, value_src, query_gain, key_gain)
    arrived = lax.all_to_all(outgoing, "seq", split_axis=0, concat_axis=0, tiled=True)
    queries = norm_up(up_query, up_gain, (0, PEER, far, far ^ PEER), nears)
    queries = dict(zip(nears, queries))
    for near in nears[1:]:
        queries[near] = swapped(queries[near], near)
    memory = short_attention(arrived, query_gain, key_gain)
    far_memory = swapped(memory, far)
    offsets, pieces = [], []
    for kind, held in enumerate((memory, far_memory)):
        peer_memory = swapped(held, PEER)
        done = attend(nears, held, 2 * kind, queries, None)
        done = attend(nears, peer_memory, 2 * kind + 1, queries, done)
        for near in nears:
            pieces.append(swapped(done[near], near) if near else done[near])
            offsets.append(near ^ (kind * far))
    return place(tuple(offsets), pieces)


def local(*arrays):
    whole = lax.axis_size("seq") == HEADS and HEADS & (HEADS - 1) == 0
    return half_exchange(*arrays) if whole else head_exchange(*arrays)


def solution(mesh):
    in_specs = (
        P(("groups", "seq"), None),
        P(("groups", "seq"), None),
        P(("groups", "seq"), None),
        P(("groups", "seq"), None),
        P(),
        P(),
        P(),
    )
    out_specs = P(("groups", "seq"), None)
    return jax.shard_map(local, mesh=mesh, in_specs=in_specs, out_specs=out_specs, check_vma=False)
```

```python
import functools
import math

import jax
import jax.numpy as jnp
from jax import lax
from jax.experimental import pallas as pl
from jax.experimental.pallas import tpu as pltpu
from jax.sharding import PartitionSpec as P


HEADS = 16
HDIM = 128
SHORT = 4
SHIFT = 3


epsilon = 1e-06


def shifted(value, axis, steps):
    count = lax.axis_size(axis)
    leading, last = (max(0, -steps), min(count, count - steps))
    return lax.ppermute(value, axis, [(source, source + steps) for source in range(leading, last)])


def head_norm(values, gain_vector):
    row_count = values.shape[0]
    by_head = values.reshape(row_count, HEADS, HDIM)
    inverse_rms = lax.rsqrt(jnp.mean(by_head * by_head, axis=2, keepdims=True) + epsilon)
    return (by_head * inverse_rms * gain_vector.reshape(1, HEADS, HDIM)).reshape(
        row_count, HEADS * HDIM
    )


def row_norm(values):
    return values * lax.rsqrt(jnp.mean(values * values, axis=-1, keepdims=True) + epsilon)


def pooled_rows(source, edge_rows):
    widened = jnp.concatenate([edge_rows, source[: source.shape[0] - SHIFT]], axis=0).astype(
        jnp.float32
    )
    return jnp.mean(widened.reshape(-1, SHORT, widened.shape[1]), axis=1)


def blocked_attention(queries, query_limit, key_rows, value_rows, key_positions, block_size):
    head_count, query_count, head_size = queries.shape
    block_total = key_rows.shape[1] // block_size
    ceiling = jnp.max(query_limit)

    def visit_block(block_index, totals):
        offset = block_index * block_size
        block_pos = lax.dynamic_slice_in_dim(key_positions, offset, block_size, 0)

        def compute(state):
            numer_in, denom_in = state
            key_block = lax.dynamic_slice_in_dim(key_rows, offset, block_size, 1)
            value_block = lax.dynamic_slice_in_dim(value_rows, offset, block_size, 1)
            scores = jnp.einsum(
                "hqd,hkd->hqk", queries, key_block, preferred_element_type=jnp.float32
            ) / math.sqrt(HDIM)
            visible = block_pos[None, :] <= query_limit[:, None]
            exponent = jnp.where(visible[None], jnp.exp(scores), 0.0)
            denom_out = denom_in + jnp.sum(exponent, axis=2)
            numer_out = numer_in + jnp.einsum(
                "hqk,hkd->hqd",
                exponent.astype(jnp.bfloat16),
                value_block,
                preferred_element_type=jnp.float32,
            )
            return (numer_out, denom_out)

        return lax.cond(jnp.min(block_pos) <= ceiling, compute, lambda state: state, totals)

    initial = (
        jnp.zeros((head_count, query_count, head_size), jnp.float32),
        jnp.zeros((head_count, query_count), jnp.float32),
    )
    numerator, denominator = lax.fori_loop(0, block_total, visit_block, initial)
    return numerator / denominator[:, :, None]


def spread_heads(matrices, row_count, block_count, device_count):
    count = len(matrices)
    joined = jnp.stack(matrices).reshape(count, row_count, HEADS, HDIM)
    joined = jnp.transpose(joined, (2, 0, 1, 3)).reshape(HEADS, 1, count * row_count, HDIM)
    return jnp.broadcast_to(joined, (HEADS, block_count, count * row_count, HDIM)).reshape(
        device_count, count * row_count, HDIM
    )


def split_pieces(matrix, row_count, block_count, device_count):
    piece = row_count // block_count
    parted = matrix.reshape(block_count, piece, HEADS, HDIM)
    return jnp.transpose(parted, (2, 0, 1, 3)).reshape(device_count, piece, HDIM)


def head_exchange(query_src, key_src, value_src, up_query, query_gain, key_gain, up_gain):
    device_count = lax.axis_size("seq")
    device_index = lax.axis_index("seq")
    block_count = device_count // HEADS
    block_index = device_index % block_count
    token_count = query_src.shape[0]
    edges = jnp.stack(
        [
            query_src[token_count - SHIFT :],
            key_src[token_count - SHIFT :],
            value_src[token_count - SHIFT :],
        ]
    )
    edges = shifted(edges, "seq", 1)
    short_query = head_norm(pooled_rows(query_src, edges[0]), query_gain).astype(jnp.bfloat16)
    short_key = head_norm(pooled_rows(key_src, edges[1]), key_gain).astype(jnp.bfloat16)
    short_value = pooled_rows(value_src, edges[2]).astype(jnp.bfloat16)
    row_count = short_query.shape[0]
    up_heads = head_norm(up_query.astype(jnp.float32), up_gain).astype(jnp.bfloat16)
    row_total = row_count * device_count
    key_block = math.gcd(512, row_total)
    row_positions = jnp.arange(row_total, dtype=jnp.int32)
    device_rows = jnp.arange(device_count, dtype=jnp.int32)[:, None]
    qkv_out = spread_heads(
        [short_query, short_key, short_value], row_count, block_count, device_count
    )
    up_out = split_pieces(up_heads, token_count, block_count, device_count)
    arrived, own_up = (
        lax.all_to_all(qkv_out, "seq", split_axis=0, concat_axis=0, tiled=True),
        lax.all_to_all(up_out, "seq", split_axis=0, concat_axis=0, tiled=True),
    )
    all_query = arrived[:, :row_count].reshape(row_total, HDIM)
    all_key = arrived[:, row_count : 2 * row_count].reshape(row_total, HDIM)
    all_value = arrived[:, 2 * row_count :].reshape(row_total, HDIM)

    def fill_block(index_now, memory_now):
        offset = index_now * key_block
        block_query = lax.dynamic_slice_in_dim(all_query, offset, key_block, 0)[None]
        limits = offset + jnp.arange(key_block, dtype=jnp.int32)
        attended = blocked_attention(
            block_query, limits, all_key[None], all_value[None], row_positions, key_block
        )[0]
        return lax.dynamic_update_slice_in_dim(
            memory_now, row_norm(attended).astype(jnp.bfloat16), offset, 0
        )

    memory = lax.fori_loop(
        0, row_total // key_block, fill_block, jnp.zeros((row_total, HDIM), jnp.bfloat16)
    )
    token_piece = token_count // block_count
    own_tokens = (
        device_rows * token_count
        + block_index * token_piece
        + jnp.arange(token_piece, dtype=jnp.int32)[None, :]
    ).reshape(-1)
    own_up = own_up.reshape(1, device_count * token_piece, HDIM)
    result = blocked_attention(
        own_up, own_tokens // SHORT, memory[None], memory[None], row_positions, key_block
    )[0]
    result = result.astype(jnp.bfloat16).reshape(device_count, token_piece, HDIM)
    returned = lax.all_to_all(result, "seq", split_axis=0, concat_axis=0, tiled=True)
    output_heads = returned.reshape(HEADS, token_count, HDIM)
    return jnp.transpose(output_heads, (1, 0, 2)).reshape(token_count, HEADS * HDIM)


EDGE_ROWS = 3 * SHIFT - 1
PEER = 1
ORDER = tuple(index ^ (HEADS - 5) for index in range(HEADS))


def rms_rows(values):
    return values * lax.rsqrt(jnp.mean(values * values, axis=-1, keepdims=True) + epsilon)


def on_chip(value):
    return pltpu.with_memory_space_constraint(value, pltpu.VMEM)


def select_matrix(tokens, rows, slot):
    row = lax.broadcasted_iota(jnp.int32, (rows + EDGE_ROWS, tokens), 0)
    col = lax.broadcasted_iota(jnp.int32, (rows + EDGE_ROWS, tokens), 1)
    pooled = (row < rows) & (col <= SHORT * row) & (col >= SHORT * row - SHIFT)
    weight = jnp.where(row == 0, 1.0, 1.0 / SHORT)
    edge = (row >= rows + slot * SHIFT) & (row < rows + (slot + 1) * SHIFT)
    last = col >= tokens - SHIFT
    if slot < 2:
        last = col == tokens - SHIFT + row - rows - slot * SHIFT
    return jnp.where(pooled, weight, jnp.where(edge & last, 1.0, 0.0)).astype(jnp.bfloat16)


def pool_kernel(*refs):
    sources, out_hbm = refs[:5], refs[5]
    buffers, out_ref, in_sems, out_sems = refs[6:11], refs[11], refs[12], refs[13]
    tokens, columns = sources[0].shape
    rows = tokens // SHORT
    copies = [
        pltpu.make_async_copy(source, buffer, in_sems.at[index])
        for index, (source, buffer) in enumerate(zip(sources, buffers))
    ]
    for index in (0, 3, 1, 4, 2):
        copies[index].start()
    picks = [select_matrix(tokens, rows, slot) for slot in range(3)]
    first = lax.broadcasted_iota(jnp.int32, (rows, HDIM), 0) == 0
    rest = lax.broadcasted_iota(jnp.int32, (EDGE_ROWS, HDIM), 0) == EDGE_ROWS - 1
    edges, returns = [], []
    for slot in range(3):
        copies[slot].wait()
        if slot < 2:
            copies[3 + slot].wait()
        picked = jnp.dot(picks[slot], buffers[slot][...], preferred_element_type=jnp.float32)
        edges.append(picked[rows:])
        span = rows if slot < 2 else rows + EDGE_ROWS
        for head in range(columns // HDIM):
            inside = slice(head * HDIM, (head + 1) * HDIM)
            part = picked[:rows, inside]
            spot = ORDER.index(head)
            if slot < 2:
                gain = buffers[3 + slot][head : head + 1, :]
                part = jnp.where(first, part, rms_rows(part) * gain)
            else:
                edge = sum(values[:, inside] for values in edges)
                high = edge.astype(jnp.bfloat16)
                low = (edge - high.astype(jnp.float32)).astype(jnp.bfloat16)
                out_ref[spot, 3 * rows :, :] = jnp.where(rest, low, high)
            out_ref[spot, slot * rows : (slot + 1) * rows, :] = part.astype(jnp.bfloat16)
        target = pl.ds(slot * rows, span)
        copy = pltpu.make_async_copy(
            out_ref.at[:, target], out_hbm.at[:, target], out_sems.at[slot]
        )
        copy.start()
        returns.append(copy)
    for copy in returns:
        copy.wait()


def pool_inputs(query_src, key_src, value_src, query_gain, key_gain):
    tokens, columns = query_src.shape
    heads = columns // HDIM
    depth = 3 * (tokens // SHORT) + EDGE_ROWS
    return pl.pallas_call(
        pool_kernel,
        in_specs=[pl.BlockSpec(memory_space=pl.ANY)] * 5,
        out_specs=pl.BlockSpec(memory_space=pl.ANY),
        out_shape=jax.ShapeDtypeStruct((heads, depth, HDIM), jnp.bfloat16),
        scratch_shapes=[pltpu.VMEM((tokens, columns), jnp.bfloat16)] * 3
        + [pltpu.VMEM((heads, HDIM), jnp.float32)] * 2
        + [pltpu.VMEM((heads, depth, HDIM), jnp.bfloat16)]
        + [pltpu.SemaphoreType.DMA((5,)), pltpu.SemaphoreType.DMA((3,))],
    )(query_src, key_src, value_src, query_gain.reshape(heads, HDIM), key_gain.reshape(heads, HDIM))


def scaled_exp(scores):
    return jnp.exp2(scores * (math.log2(math.e) / math.sqrt(HDIM)))


def across(left, right):
    return lax.dot_general(
        left, right, (((1,), (1,)), ((), ())), preferred_element_type=jnp.float32
    )


def short_kernel(block, arrived_ref, query_gain_ref, key_gain_ref, memory_ref):
    count, depth, _ = arrived_ref.shape
    rows = (depth - EDGE_ROWS) // 3
    total = count * rows
    head = lax.axis_index("seq")

    def arrived(first_row, size):
        blocks = [
            arrived_ref[pl.ds(ORDER.index(source), 1), first_row : first_row + size, :]
            for source in range(count)
        ]
        return jnp.concatenate(blocks, axis=0).astype(jnp.float32)

    edges = arrived(3 * rows, EDGE_ROWS)
    edge_row = lax.broadcasted_iota(jnp.int32, edges.shape, 1)
    first = lax.broadcasted_iota(jnp.int32, (count, rows, HDIM), 1) == 0
    tensors = []
    for slot, gain_ref in enumerate((query_gain_ref, key_gain_ref, None)):
        part = arrived(slot * rows, rows)
        own = (edge_row >= slot * SHIFT) & (edge_row < (slot + 1) * SHIFT)
        tail = jnp.sum(jnp.where(own, edges, 0.0), axis=1, keepdims=True)
        before = jnp.concatenate([jnp.zeros_like(tail[:1]), tail[:-1]], axis=0)
        mean = (before + part[:, :1, :]) * (1.0 / SHORT)
        if gain_ref is not None:
            mean = rms_rows(mean) * gain_ref[pl.ds(head, 1), :][None]
        part = jnp.where(first, mean, part).astype(jnp.bfloat16)
        tensors.append(part.reshape(total, HDIM))
    query, key, value = tensors
    diagonal = lax.broadcasted_iota(jnp.int32, (block, block), 1) <= lax.broadcasted_iota(
        jnp.int32, (block, block), 0
    )
    starts = range(0, total, block)
    sums = [0.0] * len(starts)
    numerators = [0.0] * len(starts)
    for index, start in enumerate(starts):
        exponent = scaled_exp(across(query[start:], key[start : start + block]))
        for later in range(index, len(starts)):
            offset = (later - index) * block
            part = exponent[offset : offset + block]
            if later == index:
                part = jnp.where(diagonal, part, 0.0)
            sums[later] += part
            numerators[later] += jnp.dot(
                part.astype(jnp.bfloat16),
                value[start : start + block],
                preferred_element_type=jnp.float32,
            )
    for index, start in enumerate(starts):
        denominator = jnp.sum(sums[index], axis=1, keepdims=True)
        memory_ref[start : start + block, :] = rms_rows(numerators[index] / denominator).astype(
            jnp.bfloat16
        )


def short_attention(arrived, query_gain, key_gain):
    count, depth, _ = arrived.shape
    row_total = count * (depth - EDGE_ROWS) // 3
    return pl.pallas_call(
        functools.partial(short_kernel, math.gcd(128, row_total)),
        out_shape=pltpu.VMEM((row_total, HDIM), jnp.bfloat16),
    )(on_chip(arrived), *[on_chip(gain.reshape(-1, HDIM)) for gain in (query_gain, key_gain)])


def norm_kernel(shifts, nears, up_ref, gain_ref, *out_refs):
    device = lax.axis_index("seq")
    for near, out_ref in zip(nears, out_refs):
        for index, shift in enumerate(shifts):
            head = device ^ near ^ shift
            columns = pl.ds(pl.multiple_of(head * HDIM, HDIM), HDIM)
            query = rms_rows(up_ref[:, columns].astype(jnp.float32)) * gain_ref[pl.ds(head, 1), :]
            out_ref[index] = query.astype(jnp.bfloat16)


def norm_up(up_query, up_gain, shifts, nears):
    tokens = up_query.shape[0]
    shape = pltpu.VMEM((len(shifts), tokens, HDIM), jnp.bfloat16)
    return pl.pallas_call(
        functools.partial(norm_kernel, shifts, nears), out_shape=[shape] * len(nears)
    )(up_query, up_gain.reshape(-1, HDIM))


def attend_kernel(nears, slot, *refs):
    count = len(nears)
    memory_ref, query_refs, refs = refs[0], refs[1 : count + 1], refs[count + 1 :]
    done_refs, out_refs = refs[:-count], refs[-count:]
    tokens = query_refs[0].shape[1]
    row_total = memory_ref.shape[0]
    device = lax.axis_index("seq")

    def attend_rows(rows):
        memory = memory_ref[:rows]
        token = lax.broadcasted_iota(jnp.int32, (tokens, rows), 0)
        behind = SHORT * lax.broadcasted_iota(jnp.int32, (tokens, rows), 1) - token
        query = jnp.concatenate([query_ref[slot] for query_ref in query_refs], axis=0)
        exponent = scaled_exp(across(query, memory))
        exponent = jnp.concatenate(
            [
                jnp.where(
                    behind <= (device ^ near) * tokens,
                    exponent[order * tokens : (order + 1) * tokens],
                    0.0,
                )
                for order, near in enumerate(nears)
            ],
            axis=0,
        )
        denominator = jnp.sum(exponent, axis=1, keepdims=True)
        numerator = jnp.dot(
            exponent.astype(jnp.bfloat16), memory, preferred_element_type=jnp.float32
        )
        result = (numerator / denominator).astype(jnp.bfloat16)
        for order, out_ref in enumerate(out_refs):
            out_ref[out_ref.shape[0] - 1] = result[order * tokens : (order + 1) * tokens]

    @pl.when(device < HEADS // 2)
    def _():
        attend_rows(row_total // 2)

    @pl.when(device >= HEADS // 2)
    def _():
        attend_rows(row_total)

    for done_ref, out_ref in zip(done_refs, out_refs):
        out_ref[: done_ref.shape[0]] = done_ref[...]


def attend(nears, memory, slot, queries, done):
    tokens = queries[nears[0]].shape[1]
    operands = [memory, *[queries[near] for near in nears]]
    operands += [done[near] for near in nears] if done else []
    shape = pltpu.VMEM((2 if done else 1, tokens, HDIM), jnp.bfloat16)
    results = pl.pallas_call(
        functools.partial(attend_kernel, nears, slot), out_shape=[shape] * len(nears)
    )(*[on_chip(value) for value in operands])
    return dict(zip(nears, results))


def place_kernel(offsets, *refs):
    piece_refs, out_hbm, sems = refs[:-2], refs[-2], refs[-1]
    device = lax.axis_index("seq")
    copies = []
    for number, (offset, piece_ref) in enumerate(zip(offsets, piece_refs)):
        for flip in (0, PEER):
            head = device ^ offset ^ flip
            columns = pl.ds(pl.multiple_of(head * HDIM, HDIM), HDIM)
            copy = pltpu.make_async_copy(
                piece_ref.at[flip], out_hbm.at[:, columns], sems.at[2 * number + flip]
            )
            copy.start()
            copies.append(copy)
    for copy in copies:
        copy.wait()


def place(offsets, pieces):
    return pl.pallas_call(
        functools.partial(place_kernel, offsets),
        out_specs=pl.BlockSpec(memory_space=pl.ANY),
        out_shape=jax.ShapeDtypeStruct((pieces[0].shape[1], HEADS * HDIM), jnp.bfloat16),
        scratch_shapes=[pltpu.SemaphoreType.DMA((2 * len(pieces),))],
    )(*[on_chip(piece) for piece in pieces])


def swapped(value, offset):
    count = lax.axis_size("seq")
    return lax.ppermute(value, "seq", [(source, source ^ offset) for source in range(count)])


def half_exchange(query_src, key_src, value_src, up_query, query_gain, key_gain, up_gain):
    far = HEADS // 2 + HEADS // 4
    nears = tuple(range(0, HEADS // 2, 2))
    outgoing = pool_inputs(query_src, key_src, value_src, query_gain, key_gain)
    arrived = lax.all_to_all(
        outgoing,
        "seq",
        split_axis=0,
        concat_axis=0,
        tiled=True,
        axis_index_groups=[list(ORDER)],
    )
    queries = norm_up(up_query, up_gain, (0, PEER, far, far ^ PEER), nears)
    queries = dict(zip(nears, queries))
    for near in nears[1:]:
        queries[near] = swapped(queries[near], near)
    memory = short_attention(arrived, query_gain, key_gain)
    far_memory = swapped(memory, far)
    offsets, pieces = [], []
    for kind, held in enumerate((memory, far_memory)):
        peer_memory = swapped(held, PEER)
        done = attend(nears, held, 2 * kind, queries, None)
        done = attend(nears, peer_memory, 2 * kind + 1, queries, done)
        for near in nears:
            pieces.append(swapped(done[near], near) if near else done[near])
            offsets.append(near ^ (kind * far))
    return place(tuple(offsets), pieces)


def local(*arrays):
    whole = lax.axis_size("seq") == HEADS and HEADS & (HEADS - 1) == 0
    return half_exchange(*arrays) if whole else head_exchange(*arrays)


def solution(mesh):
    in_specs = (
        P(("groups", "seq"), None),
        P(("groups", "seq"), None),
        P(("groups", "seq"), None),
        P(("groups", "seq"), None),
        P(),
        P(),
        P(),
    )
    out_specs = P(("groups", "seq"), None)
    return jax.shard_map(local, mesh=mesh, in_specs=in_specs, out_specs=out_specs, check_vma=False)
```

```python
import functools
import math

import jax
import jax.numpy as jnp
from jax import lax
from jax.experimental import pallas as pl
from jax.experimental.pallas import tpu as pltpu
from jax.sharding import PartitionSpec as P


HEADS = 16
HDIM = 128
SHORT = 4
SHIFT = 3


epsilon = 1e-06


def shifted(value, axis, steps):
    count = lax.axis_size(axis)
    leading, last = (max(0, -steps), min(count, count - steps))
    return lax.ppermute(value, axis, [(source, source + steps) for source in range(leading, last)])


def head_norm(values, gain_vector):
    row_count = values.shape[0]
    by_head = values.reshape(row_count, HEADS, HDIM)
    inverse_rms = lax.rsqrt(jnp.mean(by_head * by_head, axis=2, keepdims=True) + epsilon)
    return (by_head * inverse_rms * gain_vector.reshape(1, HEADS, HDIM)).reshape(
        row_count, HEADS * HDIM
    )


def row_norm(values):
    return values * lax.rsqrt(jnp.mean(values * values, axis=-1, keepdims=True) + epsilon)


def pooled_rows(source, edge_rows):
    widened = jnp.concatenate([edge_rows, source[: source.shape[0] - SHIFT]], axis=0).astype(
        jnp.float32
    )
    return jnp.mean(widened.reshape(-1, SHORT, widened.shape[1]), axis=1)


def blocked_attention(queries, query_limit, key_rows, value_rows, key_positions, block_size):
    head_count, query_count, head_size = queries.shape
    block_total = key_rows.shape[1] // block_size
    ceiling = jnp.max(query_limit)

    def visit_block(block_index, totals):
        offset = block_index * block_size
        block_pos = lax.dynamic_slice_in_dim(key_positions, offset, block_size, 0)

        def compute(state):
            numer_in, denom_in = state
            key_block = lax.dynamic_slice_in_dim(key_rows, offset, block_size, 1)
            value_block = lax.dynamic_slice_in_dim(value_rows, offset, block_size, 1)
            scores = jnp.einsum(
                "hqd,hkd->hqk", queries, key_block, preferred_element_type=jnp.float32
            ) / math.sqrt(HDIM)
            visible = block_pos[None, :] <= query_limit[:, None]
            exponent = jnp.where(visible[None], jnp.exp(scores), 0.0)
            denom_out = denom_in + jnp.sum(exponent, axis=2)
            numer_out = numer_in + jnp.einsum(
                "hqk,hkd->hqd",
                exponent.astype(jnp.bfloat16),
                value_block,
                preferred_element_type=jnp.float32,
            )
            return (numer_out, denom_out)

        return lax.cond(jnp.min(block_pos) <= ceiling, compute, lambda state: state, totals)

    initial = (
        jnp.zeros((head_count, query_count, head_size), jnp.float32),
        jnp.zeros((head_count, query_count), jnp.float32),
    )
    numerator, denominator = lax.fori_loop(0, block_total, visit_block, initial)
    return numerator / denominator[:, :, None]


def spread_heads(matrices, row_count, block_count, device_count):
    count = len(matrices)
    joined = jnp.stack(matrices).reshape(count, row_count, HEADS, HDIM)
    joined = jnp.transpose(joined, (2, 0, 1, 3)).reshape(HEADS, 1, count * row_count, HDIM)
    return jnp.broadcast_to(joined, (HEADS, block_count, count * row_count, HDIM)).reshape(
        device_count, count * row_count, HDIM
    )


def split_pieces(matrix, row_count, block_count, device_count):
    piece = row_count // block_count
    parted = matrix.reshape(block_count, piece, HEADS, HDIM)
    return jnp.transpose(parted, (2, 0, 1, 3)).reshape(device_count, piece, HDIM)


def head_exchange(query_src, key_src, value_src, up_query, query_gain, key_gain, up_gain):
    device_count = lax.axis_size("seq")
    device_index = lax.axis_index("seq")
    block_count = device_count // HEADS
    block_index = device_index % block_count
    token_count = query_src.shape[0]
    edges = jnp.stack(
        [
            query_src[token_count - SHIFT :],
            key_src[token_count - SHIFT :],
            value_src[token_count - SHIFT :],
        ]
    )
    edges = shifted(edges, "seq", 1)
    short_query = head_norm(pooled_rows(query_src, edges[0]), query_gain).astype(jnp.bfloat16)
    short_key = head_norm(pooled_rows(key_src, edges[1]), key_gain).astype(jnp.bfloat16)
    short_value = pooled_rows(value_src, edges[2]).astype(jnp.bfloat16)
    row_count = short_query.shape[0]
    up_heads = head_norm(up_query.astype(jnp.float32), up_gain).astype(jnp.bfloat16)
    row_total = row_count * device_count
    key_block = math.gcd(512, row_total)
    row_positions = jnp.arange(row_total, dtype=jnp.int32)
    device_rows = jnp.arange(device_count, dtype=jnp.int32)[:, None]
    qkv_out = spread_heads(
        [short_query, short_key, short_value], row_count, block_count, device_count
    )
    up_out = split_pieces(up_heads, token_count, block_count, device_count)
    arrived, own_up = (
        lax.all_to_all(qkv_out, "seq", split_axis=0, concat_axis=0, tiled=True),
        lax.all_to_all(up_out, "seq", split_axis=0, concat_axis=0, tiled=True),
    )
    all_query = arrived[:, :row_count].reshape(row_total, HDIM)
    all_key = arrived[:, row_count : 2 * row_count].reshape(row_total, HDIM)
    all_value = arrived[:, 2 * row_count :].reshape(row_total, HDIM)

    def fill_block(index_now, memory_now):
        offset = index_now * key_block
        block_query = lax.dynamic_slice_in_dim(all_query, offset, key_block, 0)[None]
        limits = offset + jnp.arange(key_block, dtype=jnp.int32)
        attended = blocked_attention(
            block_query, limits, all_key[None], all_value[None], row_positions, key_block
        )[0]
        return lax.dynamic_update_slice_in_dim(
            memory_now, row_norm(attended).astype(jnp.bfloat16), offset, 0
        )

    memory = lax.fori_loop(
        0, row_total // key_block, fill_block, jnp.zeros((row_total, HDIM), jnp.bfloat16)
    )
    token_piece = token_count // block_count
    own_tokens = (
        device_rows * token_count
        + block_index * token_piece
        + jnp.arange(token_piece, dtype=jnp.int32)[None, :]
    ).reshape(-1)
    own_up = own_up.reshape(1, device_count * token_piece, HDIM)
    result = blocked_attention(
        own_up, own_tokens // SHORT, memory[None], memory[None], row_positions, key_block
    )[0]
    result = result.astype(jnp.bfloat16).reshape(device_count, token_piece, HDIM)
    returned = lax.all_to_all(result, "seq", split_axis=0, concat_axis=0, tiled=True)
    output_heads = returned.reshape(HEADS, token_count, HDIM)
    return jnp.transpose(output_heads, (1, 0, 2)).reshape(token_count, HEADS * HDIM)


EDGE_ROWS = 3 * SHIFT - 1
PEER = 1
ORDER = tuple(index ^ (HEADS - 5) for index in range(HEADS))


def rms_rows(values):
    return values * lax.rsqrt(jnp.mean(values * values, axis=-1, keepdims=True) + epsilon)


def on_chip(value):
    return pltpu.with_memory_space_constraint(value, pltpu.VMEM)


def select_matrix(tokens, rows, slot):
    row = lax.broadcasted_iota(jnp.int32, (rows + EDGE_ROWS, tokens), 0)
    col = lax.broadcasted_iota(jnp.int32, (rows + EDGE_ROWS, tokens), 1)
    pooled = (row < rows) & (col <= SHORT * row) & (col >= SHORT * row - SHIFT)
    weight = jnp.where(row == 0, 1.0, 1.0 / SHORT)
    edge = (row >= rows + slot * SHIFT) & (row < rows + (slot + 1) * SHIFT)
    last = col >= tokens - SHIFT
    if slot < 2:
        last = col == tokens - SHIFT + row - rows - slot * SHIFT
    return jnp.where(pooled, weight, jnp.where(edge & last, 1.0, 0.0)).astype(jnp.bfloat16)


def pool_kernel(*refs):
    sources, out_hbm = refs[:5], refs[5]
    buffers, out_ref, in_sems, out_sems = refs[6:11], refs[11], refs[12], refs[13]
    tokens, columns = sources[0].shape
    rows = tokens // SHORT
    copies = [
        pltpu.make_async_copy(source, buffer, in_sems.at[index])
        for index, (source, buffer) in enumerate(zip(sources, buffers))
    ]
    for index in (0, 3, 1, 4, 2):
        copies[index].start()
    picks = [select_matrix(tokens, rows, slot) for slot in range(3)]
    first = lax.broadcasted_iota(jnp.int32, (rows, HDIM), 0) == 0
    rest = lax.broadcasted_iota(jnp.int32, (EDGE_ROWS, HDIM), 0) == EDGE_ROWS - 1
    edges, returns = [], []
    for slot in range(3):
        copies[slot].wait()
        if slot < 2:
            copies[3 + slot].wait()
        picked = jnp.dot(picks[slot], buffers[slot][...], preferred_element_type=jnp.float32)
        edges.append(picked[rows:])
        span = rows if slot < 2 else rows + EDGE_ROWS
        for head in range(columns // HDIM):
            inside = slice(head * HDIM, (head + 1) * HDIM)
            part = picked[:rows, inside]
            spot = ORDER.index(head)
            if slot < 2:
                gain = buffers[3 + slot][head : head + 1, :]
                part = jnp.where(first, part, rms_rows(part) * gain)
            else:
                edge = sum(values[:, inside] for values in edges)
                high = edge.astype(jnp.bfloat16)
                low = (edge - high.astype(jnp.float32)).astype(jnp.bfloat16)
                out_ref[spot, 3 * rows :, :] = jnp.where(rest, low, high)
            out_ref[spot, slot * rows : (slot + 1) * rows, :] = part.astype(jnp.bfloat16)
        target = pl.ds(slot * rows, span)
        copy = pltpu.make_async_copy(
            out_ref.at[:, target], out_hbm.at[:, target], out_sems.at[slot]
        )
        copy.start()
        returns.append(copy)
    for copy in returns:
        copy.wait()


def pool_inputs(query_src, key_src, value_src, query_gain, key_gain):
    tokens, columns = query_src.shape
    heads = columns // HDIM
    depth = 3 * (tokens // SHORT) + EDGE_ROWS
    return pl.pallas_call(
        pool_kernel,
        in_specs=[pl.BlockSpec(memory_space=pl.ANY)] * 5,
        out_specs=pl.BlockSpec(memory_space=pl.ANY),
        out_shape=jax.ShapeDtypeStruct((heads, depth, HDIM), jnp.bfloat16),
        scratch_shapes=[pltpu.VMEM((tokens, columns), jnp.bfloat16)] * 3
        + [pltpu.VMEM((heads, HDIM), jnp.float32)] * 2
        + [pltpu.VMEM((heads, depth, HDIM), jnp.bfloat16)]
        + [pltpu.SemaphoreType.DMA((5,)), pltpu.SemaphoreType.DMA((3,))],
    )(query_src, key_src, value_src, query_gain.reshape(heads, HDIM), key_gain.reshape(heads, HDIM))


def scaled_exp(scores):
    return jnp.exp2(scores * (math.log2(math.e) / math.sqrt(HDIM)))


def across(left, right):
    return lax.dot_general(
        left, right, (((1,), (1,)), ((), ())), preferred_element_type=jnp.float32
    )


def short_kernel(block, arrived_ref, query_gain_ref, key_gain_ref, memory_ref):
    count, depth, _ = arrived_ref.shape
    rows = (depth - EDGE_ROWS) // 3
    total = count * rows
    head = lax.axis_index("seq")

    def arrived(first_row, size):
        blocks = [
            arrived_ref[pl.ds(ORDER.index(source), 1), first_row : first_row + size, :]
            for source in range(count)
        ]
        return jnp.concatenate(blocks, axis=0).astype(jnp.float32)

    edges = arrived(3 * rows, EDGE_ROWS)
    edge_row = lax.broadcasted_iota(jnp.int32, edges.shape, 1)
    first = lax.broadcasted_iota(jnp.int32, (count, rows, HDIM), 1) == 0
    tensors = []
    for slot, gain_ref in enumerate((query_gain_ref, key_gain_ref, None)):
        part = arrived(slot * rows, rows)
        own = (edge_row >= slot * SHIFT) & (edge_row < (slot + 1) * SHIFT)
        tail = jnp.sum(jnp.where(own, edges, 0.0), axis=1, keepdims=True)
        before = jnp.concatenate([jnp.zeros_like(tail[:1]), tail[:-1]], axis=0)
        mean = (before + part[:, :1, :]) * (1.0 / SHORT)
        if gain_ref is not None:
            mean = rms_rows(mean) * gain_ref[pl.ds(head, 1), :][None]
        part = jnp.where(first, mean, part).astype(jnp.bfloat16)
        tensors.append(part.reshape(total, HDIM))
    query, key, value = tensors
    diagonal = lax.broadcasted_iota(jnp.int32, (block, block), 1) <= lax.broadcasted_iota(
        jnp.int32, (block, block), 0
    )
    starts = range(0, total, block)
    sums = [0.0] * len(starts)
    numerators = [0.0] * len(starts)
    for index, start in enumerate(starts):
        exponent = scaled_exp(across(query[start:], key[start : start + block]))
        for later in range(index, len(starts)):
            offset = (later - index) * block
            part = exponent[offset : offset + block]
            if later == index:
                part = jnp.where(diagonal, part, 0.0)
            sums[later] += part
            numerators[later] += jnp.dot(
                part.astype(jnp.bfloat16),
                value[start : start + block],
                preferred_element_type=jnp.float32,
            )
    for index, start in enumerate(starts):
        denominator = jnp.sum(sums[index], axis=1, keepdims=True)
        memory_ref[start : start + block, :] = rms_rows(numerators[index] / denominator).astype(
            jnp.bfloat16
        )


def short_attention(arrived, query_gain, key_gain):
    count, depth, _ = arrived.shape
    row_total = count * (depth - EDGE_ROWS) // 3
    return pl.pallas_call(
        functools.partial(short_kernel, math.gcd(256, row_total)),
        out_shape=pltpu.VMEM((row_total, HDIM), jnp.bfloat16),
    )(on_chip(arrived), *[on_chip(gain.reshape(-1, HDIM)) for gain in (query_gain, key_gain)])


def norm_kernel(shifts, nears, up_ref, gain_ref, *out_refs):
    device = lax.axis_index("seq")
    for near, out_ref in zip(nears, out_refs):
        for index, shift in enumerate(shifts):
            head = device ^ near ^ shift
            columns = pl.ds(pl.multiple_of(head * HDIM, HDIM), HDIM)
            query = rms_rows(up_ref[:, columns].astype(jnp.float32)) * gain_ref[pl.ds(head, 1), :]
            out_ref[index] = query.astype(jnp.bfloat16)


def norm_up(up_query, up_gain, shifts, nears):
    tokens = up_query.shape[0]
    shape = pltpu.VMEM((len(shifts), tokens, HDIM), jnp.bfloat16)
    return pl.pallas_call(
        functools.partial(norm_kernel, shifts, nears), out_shape=[shape] * len(nears)
    )(up_query, up_gain.reshape(-1, HDIM))


def attend_kernel(nears, slot, *refs):
    count = len(nears)
    memory_ref, query_refs, refs = refs[0], refs[1 : count + 1], refs[count + 1 :]
    done_refs, out_refs = refs[:-count], refs[-count:]
    tokens = query_refs[0].shape[1]
    row_total = memory_ref.shape[0]
    device = lax.axis_index("seq")

    def attend_rows(rows):
        memory = memory_ref[:rows]
        token = lax.broadcasted_iota(jnp.int32, (tokens, rows), 0)
        behind = SHORT * lax.broadcasted_iota(jnp.int32, (tokens, rows), 1) - token
        query = jnp.concatenate([query_ref[slot] for query_ref in query_refs], axis=0)
        exponent = scaled_exp(across(query, memory))
        exponent = jnp.concatenate(
            [
                jnp.where(
                    behind <= (device ^ near) * tokens,
                    exponent[order * tokens : (order + 1) * tokens],
                    0.0,
                )
                for order, near in enumerate(nears)
            ],
            axis=0,
        )
        denominator = jnp.sum(exponent, axis=1, keepdims=True)
        numerator = jnp.dot(
            exponent.astype(jnp.bfloat16), memory, preferred_element_type=jnp.float32
        )
        result = (numerator / denominator).astype(jnp.bfloat16)
        for order, out_ref in enumerate(out_refs):
            out_ref[out_ref.shape[0] - 1] = result[order * tokens : (order + 1) * tokens]

    @pl.when(device < HEADS // 2)
    def _():
        attend_rows(row_total // 2)

    @pl.when(device >= HEADS // 2)
    def _():
        attend_rows(row_total)

    for done_ref, out_ref in zip(done_refs, out_refs):
        out_ref[: done_ref.shape[0]] = done_ref[...]


def attend(nears, memory, slot, queries, done):
    tokens = queries[nears[0]].shape[1]
    operands = [memory, *[queries[near] for near in nears]]
    operands += [done[near] for near in nears] if done else []
    shape = pltpu.VMEM((2 if done else 1, tokens, HDIM), jnp.bfloat16)
    results = pl.pallas_call(
        functools.partial(attend_kernel, nears, slot), out_shape=[shape] * len(nears)
    )(*[on_chip(value) for value in operands])
    return dict(zip(nears, results))


def place_kernel(offsets, *refs):
    piece_refs, out_hbm, sems = refs[: len(offsets)], refs[-2], refs[-1]
    device = lax.axis_index("seq")
    copies = []
    for number, (offset, piece_ref) in enumerate(zip(offsets, piece_refs)):
        for flip in (0, PEER):
            head = device ^ offset ^ flip
            columns = pl.ds(pl.multiple_of(head * HDIM, HDIM), HDIM)
            copy = pltpu.make_async_copy(
                piece_ref.at[flip], out_hbm.at[:, columns], sems.at[2 * number + flip]
            )
            copy.start()
            copies.append(copy)
    for copy in copies:
        copy.wait()


def place(offsets, pieces, base=None):
    count = len(pieces)
    operands = [on_chip(piece) for piece in pieces]
    specs = [pl.BlockSpec(memory_space=pltpu.VMEM)] * count
    if base is not None:
        operands.append(base)
        specs.append(pl.BlockSpec(memory_space=pl.ANY))
    return pl.pallas_call(
        functools.partial(place_kernel, offsets),
        in_specs=specs,
        out_specs=pl.BlockSpec(memory_space=pl.ANY),
        out_shape=jax.ShapeDtypeStruct((pieces[0].shape[1], HEADS * HDIM), jnp.bfloat16),
        input_output_aliases={} if base is None else {count: 0},
        scratch_shapes=[pltpu.SemaphoreType.DMA((2 * count,))],
    )(*operands)


def swapped(value, offset):
    count = lax.axis_size("seq")
    return lax.ppermute(value, "seq", [(source, source ^ offset) for source in range(count)])


def half_exchange(query_src, key_src, value_src, up_query, query_gain, key_gain, up_gain):
    far = HEADS // 2 + HEADS // 4
    nears = tuple(range(0, HEADS // 2, 2))
    outgoing = pool_inputs(query_src, key_src, value_src, query_gain, key_gain)
    arrived = lax.all_to_all(
        outgoing,
        "seq",
        split_axis=0,
        concat_axis=0,
        tiled=True,
        axis_index_groups=[list(ORDER)],
    )
    queries = norm_up(up_query, up_gain, (0, PEER, far, far ^ PEER), nears)
    queries = dict(zip(nears, queries))
    for near in nears[1:]:
        queries[near] = swapped(queries[near], near)
    memory = short_attention(arrived, query_gain, key_gain)
    far_memory = swapped(memory, far)
    result = None
    for kind, held in enumerate((memory, far_memory)):
        peer_memory = swapped(held, PEER)
        done = attend(nears, held, 2 * kind, queries, None)
        done = attend(nears, peer_memory, 2 * kind + 1, queries, done)
        pieces = []
        for near in nears:
            pieces.append(swapped(done[near], near) if near else done[near])
        result = place(tuple(near ^ (kind * far) for near in nears), pieces, result)
    return result


def local(*arrays):
    whole = lax.axis_size("seq") == HEADS and HEADS & (HEADS - 1) == 0
    return half_exchange(*arrays) if whole else head_exchange(*arrays)


def solution(mesh):
    in_specs = (
        P(("groups", "seq"), None),
        P(("groups", "seq"), None),
        P(("groups", "seq"), None),
        P(("groups", "seq"), None),
        P(),
        P(),
        P(),
    )
    out_specs = P(("groups", "seq"), None)
    return jax.shard_map(local, mesh=mesh, in_specs=in_specs, out_specs=out_specs, check_vma=False)
```
